32 devices in a mesh: dp: 4 (over z), seq: 8 (over y, x, core).
Axes of the slice: x: 2, y: 2, z: 4, core: 2. Of those that a mesh axis runs over, the one named last changes fastest.
Arguments:
- query_rows: bfloat16 [4, 3072, 1024], P('dp', 'seq'), may hold values from -48 to 48
- key_rows: bfloat16 [4, 3072, 1024], P('dp', 'seq'), may hold values from -8 to 8
- value_rows: bfloat16 [4, 3072, 1024], P('dp', 'seq'), may hold values from -6 to 6
- scale_end: int32 [3072], P('seq'), may hold values from 1 to 3072, as said below
- out_weight: bfloat16 [1024, 2048], replicated, may hold values from -0.8984375 to 0.8984375
- grad_out: bfloat16 [4, 3072, 2048], P('dp', 'seq'), may hold values from -1.5 to 1.5
Outputs:
- mixed_out: bfloat16 [4, 3072, 2048], P('dp', 'seq')
- out_grad: float32 [1024, 2048], P(('dp', 'seq'))
The draws below stay inside these ranges and needn't reach their ends.
Inputs may be any that keep to these rules, and one draw needn't show every extreme that they name: scale_end is constant over each of 4 scales of consecutive tokens, equals the index one past the scale's last token (so scale_end[t] > t), never falls, and is 3072 on the last scale; the same for every image.
All inputs are finite; a program needn't handle non-finite values.
Results may differ from the reference program's by a relative error of at most 0.014.
Values may be sent and summed in bfloat16 or wider, within the bound.
No kernel may reach another device: no remote copies, remote signals or barrier semaphores. Data moves between devices by JAX's collectives and lax.ppermute only.
A program may use at most 256 MiB of HBM per device.

```python
import jax
import jax.numpy as jnp
from jax import lax

D = 2048
HEADS = 8
HEAD = 128
SCALES = 4
HD = 1024
TOKENS = 3072
IMAGES = 4


def query_key_pair(key):
    base = jax.random.fold_in(key, 7101)
    query_key, key_key = jax.random.split(base, 2)
    shape = (IMAGES, TOKENS, HD)
    key_values = jnp.clip(1.2 * jax.random.normal(key_key, shape, jnp.float32), -7.0, 7.0)
    query_values = jnp.clip(jax.random.normal(query_key, shape, jnp.float32), -6.0, 6.0)
    return (query_values, key_values)


def draw_query_rows(key, part):
    query_values, key_values = query_key_pair(key)
    return query_values.astype(jnp.bfloat16)


def draw_key_rows(key, part):
    query_values, key_values = query_key_pair(key)
    return key_values.astype(jnp.bfloat16)


def draw_scale_end(key, part):
    local_key = jax.random.fold_in(key, 7203)
    picks = jax.random.permutation(local_key, TOKENS - 1)[:SCALES - 1].astype(jnp.int32) + 1
    cuts = jnp.sort(picks)
    ends = jnp.concatenate([cuts, jnp.full((1,), TOKENS, jnp.int32)]).astype(jnp.int32)
    positions = jnp.arange(TOKENS, dtype=jnp.int32)
    chosen = jnp.where(ends[None, :] > positions[:, None], ends[None, :], TOKENS)
    return jnp.min(chosen, axis=1).astype(jnp.int32)


def level_of(own_key, extent, cuts, smallest, high):
    def one(axis_at, shards_of):
        draws = jax.random.uniform(jax.random.fold_in(jax.random.fold_in(own_key, 6), axis_at), (shards_of,), jnp.float32, smallest / len(cuts), high / len(cuts))
        return jnp.repeat(jnp.exp(draws), extent[axis_at] // shards_of).reshape((-1,) + (1,) * (len(extent) - axis_at - 1))

    factor_of = one(*cuts[0])
    for cut in cuts[1:]:
        factor_of = factor_of * one(*cut)
    return factor_of


def normal_values(stream_key, shape, spread, limit, pieces=(), kind=jnp.bfloat16):
    drawn = spread * jax.random.normal(stream_key, shape, jnp.float32)
    if pieces:
        drawn = drawn * level_of(stream_key, shape, pieces, -0.22, 0.18)
    return jnp.clip(drawn, -limit, limit).astype(kind)


def setup_inputs(seed: int = 0) -> dict:
    key_list = jax.random.split(jax.random.key(seed), 7)
    return {
        "query_rows": draw_query_rows(jax.random.fold_in(key_list[6], 71), 0),
        "key_rows": draw_key_rows(jax.random.fold_in(key_list[6], 71), 0),
        "value_rows": normal_values(key_list[2], (IMAGES, TOKENS, HD), 1.0, 6.0, ((0, 4), (1, 8))),
        "scale_end": draw_scale_end(jax.random.fold_in(key_list[6], 71), 0),
        "out_weight": jnp.clip(jax.random.uniform(key_list[4], (HD, D), jnp.float32, -0.8984375, 0.8984375), -0.8984375, 0.8984375).astype(jnp.bfloat16),
        "grad_out": normal_values(key_list[5], (IMAGES, TOKENS, D), (12.0 / (TOKENS * IMAGES) ** 0.5), 1.5, ((0, 4), (1, 8))),
    }


floor_score = -1.0e30


def reference(query_rows, key_rows, value_rows, scale_end, out_weight, grad_out):
    positions = jnp.arange(TOKENS, dtype=jnp.int32)
    visible = positions[None, :] < scale_end[:, None]

    def one_head(triple):
        query_head, key_head, value_head = triple
        scores = jnp.dot(query_head, key_head.T, preferred_element_type=jnp.float32) * (HEAD ** -0.5)
        masked = jnp.where(visible, scores, floor_score)
        row_max = jnp.max(masked, axis=1, keepdims=True)
        weights = jnp.where(visible, jnp.exp(masked - row_max), 0.0)
        row_sum = jnp.sum(weights, axis=1, keepdims=True)
        mixed_values = jnp.dot(weights.astype(jnp.bfloat16), value_head, preferred_element_type=jnp.float32)
        return (mixed_values / row_sum).astype(jnp.bfloat16)

    def split_heads(matrix):
        return matrix.reshape(TOKENS, HEADS, HEAD).transpose(1, 0, 2)

    def one_image(triple):
        query_img, key_img, value_img = triple
        outputs = lax.map(one_head, (split_heads(query_img), split_heads(key_img), split_heads(value_img)))
        return outputs.transpose(1, 0, 2).reshape(TOKENS, HD)

    attended = lax.map(one_image, (query_rows, key_rows, value_rows))
    flat_attended = attended.reshape(IMAGES * TOKENS, HD)
    mixed_out = jnp.dot(flat_attended, out_weight, preferred_element_type=jnp.float32).astype(jnp.bfloat16)
    mixed_out = mixed_out.reshape(IMAGES, TOKENS, D)
    out_grad = jnp.dot(flat_attended.T, grad_out.reshape(IMAGES * TOKENS, D), preferred_element_type=jnp.float32)
    return (mixed_out, out_grad)
```

```python
import functools

import jax
import jax.numpy as jnp
from jax import lax
from jax.experimental import pallas as pl
from jax.experimental.pallas import tpu as pltpu
from jax.sharding import PartitionSpec as P

HEAD = 128
FLOOR = -1e30
LOG2E = 1.4426950408889634


ANY = pl.BlockSpec(memory_space=pl.ANY)
VMEM = pl.BlockSpec(memory_space=pltpu.VMEM)
SMEM = pl.BlockSpec(memory_space=pltpu.SMEM)
LIMIT = 58 * 1024 * 1024


def place():
    index = lax.axis_index("seq")
    return index // 2, index % 2


def params(limit=LIMIT):
    return pltpu.CompilerParams(vmem_limit_bytes=limit)


def cut(rows_list, chips, width):
    row_count = rows_list[0].shape[0]
    count = len(rows_list)

    def kernel(*refs):
        sources, outs = refs[:count], refs[count:]
        chip, _ = place()
        for away in range(chips):
            start = pl.multiple_of((chip ^ away) * width, width)
            for i, source in enumerate(sources):
                outs[away][:, i * width : (i + 1) * width] = source[:, pl.ds(start, width)]

    shape = jax.ShapeDtypeStruct((row_count, count * width), rows_list[0].dtype)
    return pl.pallas_call(
        kernel,
        out_shape=[shape] * chips,
        in_specs=[VMEM] * count,
        out_specs=[VMEM] * chips,
        compiler_params=params(),
        name="cut",
    )(*rows_list)


def attend(queries, near, far, ends, chips, width):
    row_count = queries[0].shape[0]
    blocks = 2 * chips
    total = blocks * row_count
    heads = width // HEAD
    step_q = min(row_count, 384)
    step_k = 512 if total % 512 == 0 else row_count
    scale = float(HEAD) ** -0.5 * LOG2E

    def kernel(*refs):
        ends_s, ends_v = refs[0], refs[1]
        q_in = refs[2 : 2 + chips]
        near_in = refs[2 + chips : 2 + 2 * chips]
        far_in = refs[2 + 2 * chips : 2 + 3 * chips]
        outs = refs[2 + 3 * chips : 2 + 4 * chips]
        qbuf, kbuf, vbuf, obuf, sbuf, in_sem, out_sem = refs[2 + 4 * chips :]
        chip, core = place()
        copies = []
        for away in range(chips):
            other = chip ^ away
            copies.append(pltpu.make_async_copy(q_in[away], qbuf.at[away], in_sem.at[len(copies)]))
            for side, pieces in ((core, near_in), (1 - core, far_in)):
                rows = pl.ds(pl.multiple_of((other * 2 + side) * row_count, row_count), row_count)
                for half, target in enumerate((kbuf, vbuf)):
                    copies.append(
                        pltpu.make_async_copy(
                            pieces[away].at[:, half * width : (half + 1) * width],
                            target.at[rows, :],
                            in_sem.at[len(copies)],
                        )
                    )
        for copy in copies:
            copy.start()
        for copy in copies:
            copy.wait()

        def block(step, carry):
            away = step // (heads * (row_count // step_q))
            rest = step % (heads * (row_count // step_q))
            head = rest % heads
            first = pl.multiple_of((rest // heads) * step_q, step_q)
            columns = pl.ds(pl.multiple_of(head * HEAD, HEAD), HEAD)
            query = qbuf[away, pl.ds(first, step_q), columns]
            low = ends_s[away, first]
            high = ends_s[away, first + step_q - 1]
            full = low // step_k
            count = (high + step_k - 1) // step_k

            def scores(at):
                key = kbuf[pl.ds(pl.multiple_of(at * step_k, step_k), step_k), columns]
                return lax.dot_general(
                    query, key, (((1,), (1,)), ((), ())), preferred_element_type=jnp.float32
                )

            def keep(at, value, top):
                sbuf[:, pl.ds(pl.multiple_of(at * step_k, step_k), step_k)] = value
                for piece in range(step_k // HEAD):
                    top = jnp.maximum(top, value[:, piece * HEAD : (piece + 1) * HEAD])
                return top

            def whole_chunk(at, top):
                return keep(at, scores(at), top)

            def cut_chunk(at, top):
                position = at * step_k + lax.broadcasted_iota(jnp.int32, (step_q, step_k), 1)
                limit = ends_v[away, pl.ds(first, step_q), 0:1]
                return keep(at, jnp.where(position < limit, scores(at), FLOOR), top)

            top = jnp.full((step_q, HEAD), FLOOR, jnp.float32)
            top = lax.fori_loop(0, full, whole_chunk, top)
            top = lax.fori_loop(full, count, cut_chunk, top)
            shift = jnp.max(top, axis=1, keepdims=True) * scale

            def weigh(at, state):
                acc, tally = state
                span = pl.ds(pl.multiple_of(at * step_k, step_k), step_k)
                weights = jnp.exp2(sbuf[:, span] * scale - shift)
                for piece in range(step_k // HEAD):
                    tally = tally + weights[:, piece * HEAD : (piece + 1) * HEAD]
                acc = acc + jnp.dot(
                    weights.astype(jnp.bfloat16),
                    vbuf[span, columns],
                    preferred_element_type=jnp.float32,
                )
                return acc, tally

            zero = jnp.zeros((step_q, HEAD), jnp.float32)
            acc, tally = lax.fori_loop(0, count, weigh, (zero, zero))
            obuf[away, pl.ds(first, step_q), columns] = (
                acc / jnp.sum(tally, axis=1, keepdims=True)
            ).astype(jnp.bfloat16)
            return carry

        lax.fori_loop(0, chips * heads * (row_count // step_q), block, 0)
        copies = [
            pltpu.make_async_copy(obuf.at[away], outs[away], out_sem.at[away])
            for away in range(chips)
        ]
        for copy in copies:
            copy.start()
        for copy in copies:
            copy.wait()

    wide = jnp.broadcast_to(ends[:, :, None], (chips, row_count, HEAD))
    bf16 = jnp.bfloat16
    return pl.pallas_call(
        kernel,
        out_shape=[jax.ShapeDtypeStruct((row_count, width), bf16)] * chips,
        in_specs=[SMEM, VMEM] + [ANY] * (3 * chips),
        out_specs=[ANY] * chips,
        scratch_shapes=[
            pltpu.VMEM((chips, row_count, width), bf16),
            pltpu.VMEM((total, width), bf16),
            pltpu.VMEM((total, width), bf16),
            pltpu.VMEM((chips, row_count, width), bf16),
            pltpu.VMEM((step_q, total), jnp.float32),
            pltpu.SemaphoreType.DMA((5 * chips,)),
            pltpu.SemaphoreType.DMA((chips,)),
        ],
        compiler_params=params(),
        name="attend",
    )(ends, wide, *queries, *near, *far)


def weight_gradient(near, far, grad_near, grad_far, chips, width, planes):
    row_count = near[0].shape[0]
    full = chips * width
    out_width = grad_near.shape[1]
    group = full // (planes * chips * 2)

    def kernel(*refs):
        pieces = (refs[0:chips], refs[chips : 2 * chips])
        grads = refs[2 * chips : 2 * chips + 2]
        outs = refs[2 * chips + 2 : 3 * chips + 2]
        turned, left = refs[3 * chips + 2 :]
        chip, core = place()
        for side in range(2):
            for away in range(chips):
                start = pl.multiple_of((chip ^ away) * width, width)
                turned[pl.ds(start, width), side * row_count : (side + 1) * row_count] = (
                    pieces[side][away][...].T
                )
        for away in range(chips):
            for plane in range(planes):
                start = pl.multiple_of(
                    ((plane * chips + (chip ^ away)) * 2 + core) * group, group
                )
                left[plane * group : (plane + 1) * group, :] = turned[pl.ds(start, group), :]
            value = jnp.dot(
                left[:, :row_count], grads[0][...], preferred_element_type=jnp.float32
            ) + jnp.dot(left[:, row_count:], grads[1][...], preferred_element_type=jnp.float32)
            outs[away][...] = value.astype(outs[away].dtype)

    shapes = [
        jax.ShapeDtypeStruct((planes * group, out_width), jnp.float32 if away == 0 else jnp.bfloat16)
        for away in range(chips)
    ]
    return pl.pallas_call(
        kernel,
        out_shape=shapes,
        in_specs=[VMEM] * (2 * chips + 2),
        out_specs=[VMEM] * chips,
        scratch_shapes=[
            pltpu.VMEM((full, 2 * row_count), jnp.bfloat16),
            pltpu.VMEM((planes * group, 2 * row_count), jnp.bfloat16),
        ],
        compiler_params=params(),
        name="weight_gradient",
    )(*near, *far, grad_near, grad_far)


def project(pieces, out_weight, chips, width):
    row_count = pieces[0].shape[0]
    out_width = out_weight.shape[1]

    def kernel(*refs):
        ins, weight, out = refs[:chips], refs[chips], refs[chips + 1]
        chip, _ = place()
        step = min(out_width, 512)
        for column in range(0, out_width, step):
            value = None
            for away in range(chips):
                start = pl.multiple_of((chip ^ away) * width, width)
                part = jnp.dot(
                    ins[away][...],
                    weight[pl.ds(start, width), column : column + step],
                    preferred_element_type=jnp.float32,
                )
                value = part if value is None else value + part
            out[:, column : column + step] = value.astype(out.dtype)

    return pl.pallas_call(
        kernel,
        out_shape=jax.ShapeDtypeStruct((row_count, out_width), jnp.bfloat16),
        in_specs=[VMEM] * (chips + 1),
        out_specs=VMEM,
        compiler_params=params(),
        name="project",
    )(*pieces, out_weight)


def add_up(own, others, planes):
    group = own.shape[0] // planes

    def kernel(*refs):
        ins, outs = refs[: 1 + len(others)], refs[1 + len(others) :]
        plane = lax.axis_index("dp")
        for away in range(planes):
            rows = pl.ds(pl.multiple_of((plane ^ away) * group, group), group)
            value = ins[0][rows, :]
            for ref in ins[1:]:
                value = value + ref[rows, :].astype(jnp.float32)
            outs[away][...] = value.astype(outs[away].dtype)

    return pl.pallas_call(
        kernel,
        out_shape=[
            jax.ShapeDtypeStruct(
                (group, own.shape[1]), jnp.float32 if away == 0 else jnp.bfloat16
            )
            for away in range(planes)
        ],
        in_specs=[VMEM] * (1 + len(others)),
        out_specs=[VMEM] * planes,
        compiler_params=params(),
        name="add_up",
    )(own, *others)


def body(seq, planes, query_rows, key_rows, value_rows, scale_end, out_weight, grad_out):
    chips = seq // 2
    full = query_rows.shape[2]
    width = full // chips

    def over_seq(value, mask):
        return lax.ppermute(value, "seq", [(i, i ^ mask) for i in range(seq)])

    def over_dp(value, mask):
        return lax.ppermute(value, "dp", [(i, i ^ mask) for i in range(planes)])

    def spread(pieces):
        return [pieces[0]] + [over_seq(pieces[away], 2 * away) for away in range(1, chips)]

    near_ends = spread([scale_end] * chips)
    pairs = cut([key_rows[0], value_rows[0]], chips, width)
    near = spread(pairs)
    queries = spread(cut([query_rows[0]], chips, width))
    far = [over_seq(piece, 1) for piece in near]
    grad_near = grad_out[0]
    grad_far = over_seq(grad_near, 1)
    attended = attend(queries, near, far, jnp.stack(near_ends), chips, width)
    mine = spread(attended)
    others = [over_seq(piece, 1) for piece in mine]
    shares = weight_gradient(mine, others, grad_near, grad_far, chips, width, planes)
    arrived = spread(shares)
    mixed_out = project(mine, out_weight, chips, width)[None]
    groups = add_up(arrived[0], arrived[1:], planes)
    total = groups[0]
    for away in range(1, planes):
        total = total + over_dp(groups[away], away).astype(jnp.float32)
    return mixed_out, total


def solution(mesh):
    placed = (
        P("dp", "seq", None),
        P("dp", "seq", None),
        P("dp", "seq", None),
        P("seq"),
        P(),
        P("dp", "seq", None),
    )
    return jax.shard_map(
        functools.partial(body, mesh.shape["seq"], mesh.shape["dp"]),
        mesh=mesh,
        in_specs=placed,
        out_specs=(P("dp", "seq", None), P(("dp", "seq"), None)),
        check_vma=False,
    )
```

```python
import functools

import jax
import jax.numpy as jnp
from jax import lax
from jax.experimental import pallas as pl
from jax.experimental.pallas import tpu as pltpu
from jax.sharding import PartitionSpec as P

HEAD = 128
FLOOR = -1e30
SCALES = 4
LOG2E = 1.4426950408889634


VMEM = pl.BlockSpec(memory_space=pltpu.VMEM)
SMEM = pl.BlockSpec(memory_space=pltpu.SMEM)


def place():
    index = lax.axis_index("seq")
    return index // 2, index % 2


def params(mebibytes):
    return pltpu.CompilerParams(vmem_limit_bytes=mebibytes * 1024 * 1024)


def cut(key_rows, value_rows, query_rows, chips, width):
    row_count = key_rows.shape[0]

    def kernel(*refs):
        sources, outs = refs[:3], refs[3:]
        chip, _ = place()
        for away in range(chips):
            start = pl.multiple_of((chip ^ away) * width, width)
            columns = pl.ds(start, width)
            outs[away][:, :width] = sources[0][:, columns]
            outs[away][:, width:] = sources[1][:, columns]
            outs[chips + away][...] = sources[2][:, columns]

    kind = key_rows.dtype
    outs = pl.pallas_call(
        kernel,
        out_shape=[jax.ShapeDtypeStruct((row_count, 2 * width), kind)] * chips
        + [jax.ShapeDtypeStruct((row_count, width), kind)] * chips,
        in_specs=[VMEM] * 3,
        out_specs=[VMEM] * (2 * chips),
        compiler_params=params(16),
        name="cut",
    )(key_rows, value_rows, query_rows)
    return outs[:chips], outs[chips:]


def assemble(near, far, chips):
    row_count, wide = near[0].shape

    def kernel(*refs):
        pieces, out = (refs[:chips], refs[chips : 2 * chips]), refs[2 * chips]
        chip, core = place()
        for away in range(chips):
            for side in range(2):
                at = (chip ^ away) * 2 + (core ^ side)
                rows = pl.ds(pl.multiple_of(at * row_count, row_count), row_count)
                out[rows, :] = pieces[side][away][...]

    return pl.pallas_call(
        kernel,
        out_shape=jax.ShapeDtypeStruct((2 * chips * row_count, wide), near[0].dtype),
        in_specs=[VMEM] * (2 * chips),
        out_specs=VMEM,
        compiler_params=params(16),
        name="assemble",
    )(*near, *far)


def attend(queries, ends, aways, both, width):
    row_count = queries[0].shape[0]
    total = both.shape[0]
    heads = width // HEAD
    count = len(queries)
    choices = 4
    step_k = total // choices
    scale = float(HEAD) ** -0.5 * LOG2E

    def kernel(*refs):
        ends_in = refs[:count]
        q_in = refs[count : 2 * count]
        both_ref = refs[2 * count]
        outs = refs[2 * count + 1 : 3 * count + 1]
        qbuf, obuf, sbuf = refs[3 * count + 1 :]
        chip, core = place()

        def block(index, starts, limits, steps):
            token = starts + lax.broadcasted_iota(jnp.int32, (row_count, HEAD), 0)
            limit = jnp.full((row_count, HEAD), limits[-1], jnp.int32)
            for value in reversed(limits[:-1]):
                limit = jnp.where(token < value, value, limit)
            room = limit - lax.broadcasted_iota(jnp.int32, (row_count, HEAD), 1)
            shifts = []
            for head in range(heads):
                columns = slice(head * HEAD, (head + 1) * HEAD)
                query = qbuf[index, :, columns]
                top = None
                for at in range(0, steps * step_k, step_k):
                    score = lax.dot_general(
                        query,
                        both_ref[at : at + step_k, columns],
                        (((1,), (1,)), ((), ())),
                        preferred_element_type=jnp.float32,
                    )
                    for base in range(0, step_k, HEAD):
                        part = jnp.where(room > at + base, score[:, base : base + HEAD], FLOOR)
                        sbuf[head, :, at + base : at + base + HEAD] = part
                        top = part if top is None else jnp.maximum(top, part)
                shifts.append(jnp.max(top, axis=1, keepdims=True) * scale)
            for head in range(heads):
                columns = slice(head * HEAD, (head + 1) * HEAD)
                tally = acc = None
                for at in range(0, steps * step_k, step_k):
                    weights = jnp.exp2(sbuf[head, :, at : at + step_k] * scale - shifts[head])
                    for base in range(0, step_k, HEAD):
                        part = weights[:, base : base + HEAD]
                        tally = part if tally is None else tally + part
                    product = jnp.dot(
                        weights.astype(jnp.bfloat16),
                        both_ref[at : at + step_k, width + head * HEAD : width + (head + 1) * HEAD],
                        preferred_element_type=jnp.float32,
                    )
                    acc = product if acc is None else acc + product
                obuf[index, :, columns] = (acc / jnp.sum(tally, axis=1, keepdims=True)).astype(
                    obuf.dtype
                )

        starts, limits = [], []
        for index, away in enumerate(aways):
            qbuf[index] = q_in[index][...]
            start = ((chip ^ away) * 2 + core) * row_count
            limit = [ends_in[index][0]]
            for _ in range(SCALES - 1):
                limit.append(ends_in[index][jnp.minimum(limit[-1] - start, row_count - 1)])
            starts.append(start)
            limits.append(limit)

        def turn(index, carry):
            def pick(values):
                value = values[0]
                for at in range(1, count):
                    value = jnp.where(index == at, values[at], value)
                return value

            start = pick(starts)
            limit = [pick([one[at] for one in limits]) for at in range(SCALES)]
            needed = (limit[-1] + step_k - 1) // step_k
            for steps in range(1, choices + 1):

                @pl.when(needed == steps)
                def _(steps=steps):
                    block(index, start, limit, steps)

            return carry

        lax.fori_loop(0, count, turn, 0)
        for index in range(count):
            outs[index][...] = obuf[index]

    return pl.pallas_call(
        kernel,
        out_shape=[jax.ShapeDtypeStruct((row_count, width), jnp.bfloat16)] * count,
        in_specs=[SMEM] * count + [VMEM] * (count + 1),
        out_specs=[VMEM] * count,
        scratch_shapes=[
            pltpu.VMEM((count, row_count, width), jnp.bfloat16),
            pltpu.VMEM((count, row_count, width), jnp.bfloat16),
            pltpu.VMEM((heads, row_count, total), jnp.float32),
        ],
        compiler_params=params(30),
        cost_estimate=pl.CostEstimate(
            flops=4 * count * row_count * total * width,
            bytes_accessed=4 * total * width,
            transcendentals=count * row_count * total * heads,
        ),
        name="attend",
    )(*ends, *queries, both)


def weight_gradient(near, far, grad_near, grad_far, chips, width, planes, split):
    row_count = near[0].shape[0]
    full = chips * width
    out_width = grad_near.shape[1]
    group = full // (planes * chips * 2)

    def kernel(*refs):
        pieces = (refs[0:chips], refs[chips : 2 * chips])
        grads = refs[2 * chips : 2 * chips + 2]
        by_plane = refs[2 * chips + 2 : 2 * chips + 2 + planes]
        by_chip = refs[2 * chips + 2 + planes : 3 * chips + 2 + planes]
        turned, left = refs[3 * chips + 2 + planes :]
        chip, core = place()
        here = lax.axis_index("dp")
        for side in range(2):
            for away in range(chips):
                start = pl.multiple_of((chip ^ away) * width, width)
                turned[pl.ds(start, width), side * row_count : (side + 1) * row_count] = (
                    pieces[side][away][...].T
                )

        def product(outs, columns, picks):
            for out, starts in zip(outs, picks):
                for at, start in enumerate(starts):
                    rows = pl.ds(pl.multiple_of((start * 2 + core) * group, group), group)
                    left[at * group : (at + 1) * group, :] = turned[rows, :]
                size = len(starts) * group
                value = jnp.dot(
                    left[:size, :row_count], grads[0][:, columns], preferred_element_type=jnp.float32
                ) + jnp.dot(
                    left[:size, row_count:], grads[1][:, columns], preferred_element_type=jnp.float32
                )
                out[...] = value.astype(out.dtype)

        product(
            by_plane,
            slice(split, out_width),
            [[(here ^ far_) * chips + at for at in range(chips)] for far_ in range(planes)],
        )
        product(
            by_chip,
            slice(0, split),
            [[at * chips + (chip ^ far_) for at in range(planes)] for far_ in range(chips)],
        )

    def shape(rows, columns, away):
        return jax.ShapeDtypeStruct((rows, columns), jnp.float32 if away == 0 else jnp.bfloat16)

    outs = pl.pallas_call(
        kernel,
        out_shape=[shape(chips * group, out_width - split, away) for away in range(planes)]
        + [shape(planes * group, split, away) for away in range(chips)],
        in_specs=[VMEM] * (2 * chips + 2),
        out_specs=[VMEM] * (planes + chips),
        scratch_shapes=[
            pltpu.VMEM((full, 2 * row_count), jnp.bfloat16),
            pltpu.VMEM((max(planes, chips) * group, 2 * row_count), jnp.bfloat16),
        ],
        compiler_params=params(32),
        cost_estimate=pl.CostEstimate(
            flops=2 * full * row_count * out_width,
            bytes_accessed=4 * row_count * out_width,
            transcendentals=0,
        ),
        name="weight_gradient",
    )(*near, *far, grad_near, grad_far)
    return outs[:planes], outs[planes:]


def project(pieces, out_weight, chips, width):
    row_count = pieces[0].shape[0]
    out_width = out_weight.shape[1]

    def kernel(*refs):
        ins, weight, out = refs[:chips], refs[chips], refs[chips + 1]
        chip, _ = place()
        step = min(out_width, 512)
        for column in range(0, out_width, step):
            value = None
            for away in range(chips):
                start = pl.multiple_of((chip ^ away) * width, width)
                part = jnp.dot(
                    ins[away][...],
                    weight[pl.ds(start, width), column : column + step],
                    preferred_element_type=jnp.float32,
                )
                value = part if value is None else value + part
            out[:, column : column + step] = value.astype(out.dtype)

    return pl.pallas_call(
        kernel,
        out_shape=jax.ShapeDtypeStruct((row_count, out_width), jnp.bfloat16),
        in_specs=[VMEM] * (chips + 1),
        out_specs=VMEM,
        compiler_params=params(24),
        cost_estimate=pl.CostEstimate(
            flops=2 * row_count * out_weight.size,
            bytes_accessed=2 * out_weight.size,
            transcendentals=0,
        ),
        name="project",
    )(*pieces, out_weight)


def add_up(own, others, axis, size):
    group = own.shape[0] // size

    def kernel(*refs):
        ins, outs = refs[: 1 + len(others)], refs[1 + len(others) :]
        here = lax.axis_index("dp") if axis == "dp" else place()[0]
        for away in range(size):
            rows = pl.ds(pl.multiple_of((here ^ away) * group, group), group)
            value = ins[0][rows, :]
            for ref in ins[1:]:
                value = value + ref[rows, :].astype(jnp.float32)
            outs[away][...] = value.astype(outs[away].dtype)

    return pl.pallas_call(
        kernel,
        out_shape=[
            jax.ShapeDtypeStruct(
                (group, own.shape[1]), jnp.float32 if away == 0 else jnp.bfloat16
            )
            for away in range(size)
        ],
        in_specs=[VMEM] * (1 + len(others)),
        out_specs=[VMEM] * size,
        compiler_params=params(16),
        name="add_up",
    )(own, *others)


def body(seq, planes, query_rows, key_rows, value_rows, scale_end, out_weight, grad_out):
    chips = seq // 2
    full = query_rows.shape[2]
    width = full // chips

    def over_seq(value, mask):
        return lax.ppermute(value, "seq", [(i, i ^ mask) for i in range(seq)])

    def over_dp(value, mask):
        return lax.ppermute(value, "dp", [(i, i ^ mask) for i in range(planes)])

    def spread(pieces):
        return [pieces[0]] + [over_seq(pieces[away], 2 * away) for away in range(1, chips)]

    def meet(pieces):
        return [pieces[0]] + [over_dp(pieces[away], away) for away in range(1, planes)]

    def total(pieces):
        value = pieces[0]
        for piece in pieces[1:]:
            value = value + piece.astype(jnp.float32)
        return value

    pairs, own_queries = cut(key_rows[0], value_rows[0], query_rows[0], chips, width)
    near = spread(pairs)
    queries = spread(own_queries)
    ends = spread([scale_end] * chips)
    far = [over_seq(piece, 1) for piece in near]
    grad_near = grad_out[0]
    grad_far = over_seq(grad_near, 1)
    both = assemble(near, far, chips)
    rounds = [list(range(chips // 2)), list(range(chips // 2, chips))]
    mine = [None] * chips
    others = [None] * chips
    for aways in rounds:
        results = attend([queries[i] for i in aways], [ends[i] for i in aways], aways, both, width)
        for away, piece in zip(aways, results):
            mine[away] = over_seq(piece, 2 * away) if away else piece
            others[away] = over_seq(mine[away], 1)
    out_width = out_weight.shape[1]
    split = out_width * 5 // 8
    by_plane, by_chip = weight_gradient(
        mine, others, grad_near, grad_far, chips, width, planes, split
    )
    met = meet(by_plane)
    gathered = spread(by_chip)
    mixed_out = project(mine, out_weight, chips, width)[None]
    right = total(spread(add_up(met[0], met[1:], "seq", chips)))
    left = total(meet(add_up(gathered[0], gathered[1:], "dp", planes)))
    return mixed_out, jnp.concatenate([left, right], axis=1)


def solution(mesh):
    placed = (
        P("dp", "seq", None),
        P("dp", "seq", None),
        P("dp", "seq", None),
        P("seq"),
        P(),
        P("dp", "seq", None),
    )
    return jax.shard_map(
        functools.partial(body, mesh.shape["seq"], mesh.shape["dp"]),
        mesh=mesh,
        in_specs=placed,
        out_specs=(P("dp", "seq", None), P(("dp", "seq"), None)),
        check_vma=False,
    )
```

```python
import functools

import jax
import jax.numpy as jnp
from jax import lax
from jax.experimental import pallas as pl
from jax.experimental.pallas import tpu as pltpu
from jax.sharding import PartitionSpec as P


HEAD = 128
FLOOR = -1e30
SCALES = 4
LOG2E = 1.4426950408889634


HBM = pl.BlockSpec(memory_space=pltpu.HBM)
VMEM = pl.BlockSpec(memory_space=pltpu.VMEM)
SMEM = pl.BlockSpec(memory_space=pltpu.SMEM)


def place():
    index = lax.axis_index("seq")
    return index // 2, index % 2


def params(mebibytes):
    return pltpu.CompilerParams(vmem_limit_bytes=mebibytes * 1024 * 1024)


def cut(sources, chips, width):
    row_count = sources[0].shape[0]
    count = len(sources)

    def kernel(*refs):
        ins, outs, sems = refs[:count], refs[count:-1], refs[-1]
        chip, _ = place()
        copies = []
        for away in reversed(range(chips)):
            columns = pl.ds(pl.multiple_of((chip ^ away) * width, width), width)
            for at, source in enumerate(ins):
                copies.append(
                    pltpu.make_async_copy(
                        source.at[:, columns],
                        outs[away].at[:, at * width : (at + 1) * width],
                        sems.at[len(copies)],
                    )
                )
        for copy in copies:
            copy.start()
        for copy in copies:
            copy.wait()

    shape = jax.ShapeDtypeStruct((row_count, count * width), sources[0].dtype)
    return pl.pallas_call(
        kernel,
        out_shape=[shape] * chips,
        in_specs=[HBM] * count,
        out_specs=[VMEM] * chips,
        scratch_shapes=[pltpu.SemaphoreType.DMA((count * chips,))],
        compiler_params=params(16),
        name="cut",
    )(*sources)


def assemble(near, far, chips):
    row_count, wide = near[0].shape

    def kernel(*refs):
        pieces, out = (refs[:chips], refs[chips : 2 * chips]), refs[2 * chips]
        chip, core = place()
        for away in range(chips):
            for side in range(2):
                at = (chip ^ away) * 2 + (core ^ side)
                rows = pl.ds(pl.multiple_of(at * row_count, row_count), row_count)
                out[rows, :] = pieces[side][away][...]

    return pl.pallas_call(
        kernel,
        out_shape=jax.ShapeDtypeStruct((2 * chips * row_count, wide), near[0].dtype),
        in_specs=[VMEM] * (2 * chips),
        out_specs=VMEM,
        compiler_params=params(16),
        name="assemble",
    )(*near, *far)


def attend(queries, ends, aways, both, width):
    row_count = queries[0].shape[0]
    total = both.shape[0]
    heads = width // HEAD
    count = len(queries)
    choices = 4
    step_k = total // choices
    scale = float(HEAD) ** -0.5 * LOG2E

    def kernel(*refs):
        ends_in = refs[:count]
        q_in = refs[count : 2 * count]
        both_ref = refs[2 * count]
        outs = refs[2 * count + 1 : 3 * count + 1]
        qbuf, obuf, sbuf = refs[3 * count + 1 :]
        chip, core = place()

        def block(index, starts, limits, steps):
            token = starts + lax.broadcasted_iota(jnp.int32, (row_count, HEAD), 0)
            limit = jnp.full((row_count, HEAD), limits[-1], jnp.int32)
            for value in reversed(limits[:-1]):
                limit = jnp.where(token < value, value, limit)
            room = limit - lax.broadcasted_iota(jnp.int32, (row_count, HEAD), 1)
            shifts = []
            for head in range(heads):
                columns = slice(head * HEAD, (head + 1) * HEAD)
                query = qbuf[index, :, columns]
                top = None
                for at in range(0, steps * step_k, step_k):
                    score = lax.dot_general(
                        query,
                        both_ref[at : at + step_k, columns],
                        (((1,), (1,)), ((), ())),
                        preferred_element_type=jnp.float32,
                    )
                    for base in range(0, step_k, HEAD):
                        part = jnp.where(room > at + base, score[:, base : base + HEAD], FLOOR)
                        sbuf[head, :, at + base : at + base + HEAD] = part
                        top = part if top is None else jnp.maximum(top, part)
                shifts.append(jnp.max(top, axis=1, keepdims=True) * scale)
            for head in range(heads):
                columns = slice(head * HEAD, (head + 1) * HEAD)
                tally = acc = None
                for at in range(0, steps * step_k, step_k):
                    weights = jnp.exp2(sbuf[head, :, at : at + step_k] * scale - shifts[head])
                    for base in range(0, step_k, HEAD):
                        part = weights[:, base : base + HEAD]
                        tally = part if tally is None else tally + part
                    product = jnp.dot(
                        weights.astype(jnp.bfloat16),
                        both_ref[at : at + step_k, width + head * HEAD : width + (head + 1) * HEAD],
                        preferred_element_type=jnp.float32,
                    )
                    acc = product if acc is None else acc + product
                obuf[index, :, columns] = (acc / jnp.sum(tally, axis=1, keepdims=True)).astype(
                    obuf.dtype
                )

        starts, limits = [], []
        for index, away in enumerate(aways):
            qbuf[index] = q_in[index][...]
            start = ((chip ^ away) * 2 + core) * row_count
            limit = [ends_in[index][0]]
            for _ in range(SCALES - 1):
                limit.append(ends_in[index][jnp.minimum(limit[-1] - start, row_count - 1)])
            starts.append(start)
            limits.append(limit)

        def turn(index, carry):
            def pick(values):
                value = values[0]
                for at in range(1, count):
                    value = jnp.where(index == at, values[at], value)
                return value

            start = pick(starts)
            limit = [pick([one[at] for one in limits]) for at in range(SCALES)]
            needed = (limit[-1] + step_k - 1) // step_k
            for steps in range(1, choices + 1):

                @pl.when(needed == steps)
                def _(steps=steps):
                    block(index, start, limit, steps)

            return carry

        lax.fori_loop(0, count, turn, 0)
        for index in range(count):
            outs[index][...] = obuf[index]

    return pl.pallas_call(
        kernel,
        out_shape=[jax.ShapeDtypeStruct((row_count, width), jnp.bfloat16)] * count,
        in_specs=[SMEM] * count + [VMEM] * (count + 1),
        out_specs=[VMEM] * count,
        scratch_shapes=[
            pltpu.VMEM((count, row_count, width), jnp.bfloat16),
            pltpu.VMEM((count, row_count, width), jnp.bfloat16),
            pltpu.VMEM((heads, row_count, total), jnp.float32),
        ],
        compiler_params=params(30),
        cost_estimate=pl.CostEstimate(
            flops=4 * count * row_count * total * width,
            bytes_accessed=4 * total * width,
            transcendentals=count * row_count * total * heads,
        ),
        name="attend",
    )(*ends, *queries, both)


def weight_gradient(near, far, grad_near, grad_far, chips, width, planes, split):
    row_count = near[0].shape[0]
    full = chips * width
    out_width = grad_near.shape[1]
    group = full // (planes * chips * 2)

    def kernel(*refs):
        pieces = (refs[0:chips], refs[chips : 2 * chips])
        grads = refs[2 * chips : 2 * chips + 2]
        by_plane = refs[2 * chips + 2 : 2 * chips + 2 + planes]
        by_chip = refs[2 * chips + 2 + planes : 3 * chips + 2 + planes]
        turned, left = refs[3 * chips + 2 + planes :]
        chip, core = place()
        here = lax.axis_index("dp")
        for side in range(2):
            for away in range(chips):
                start = pl.multiple_of((chip ^ away) * width, width)
                turned[pl.ds(start, width), side * row_count : (side + 1) * row_count] = (
                    pieces[side][away][...].T
                )

        def product(outs, columns, picks):
            for out, starts in zip(outs, picks):
                for at, start in enumerate(starts):
                    rows = pl.ds(pl.multiple_of((start * 2 + core) * group, group), group)
                    left[at * group : (at + 1) * group, :] = turned[rows, :]
                size = len(starts) * group
                value = jnp.dot(
                    left[:size, :row_count], grads[0][:, columns], preferred_element_type=jnp.float32
                ) + jnp.dot(
                    left[:size, row_count:], grads[1][:, columns], preferred_element_type=jnp.float32
                )
                out[...] = value.astype(out.dtype)

        product(
            by_plane,
            slice(split, out_width),
            [[(here ^ far_) * chips + at for at in range(chips)] for far_ in range(planes)],
        )
        product(
            by_chip,
            slice(0, split),
            [[at * chips + (chip ^ far_) for at in range(planes)] for far_ in range(chips)],
        )

    def shape(rows, columns, away):
        return jax.ShapeDtypeStruct((rows, columns), jnp.float32 if away == 0 else jnp.bfloat16)

    outs = pl.pallas_call(
        kernel,
        out_shape=[shape(chips * group, out_width - split, away) for away in range(planes)]
        + [shape(planes * group, split, away) for away in range(chips)],
        in_specs=[VMEM] * (2 * chips + 2),
        out_specs=[VMEM] * (planes + chips),
        scratch_shapes=[
            pltpu.VMEM((full, 2 * row_count), jnp.bfloat16),
            pltpu.VMEM((max(planes, chips) * group, 2 * row_count), jnp.bfloat16),
        ],
        compiler_params=params(32),
        cost_estimate=pl.CostEstimate(
            flops=2 * full * row_count * out_width,
            bytes_accessed=4 * row_count * out_width,
            transcendentals=0,
        ),
        name="weight_gradient",
    )(*near, *far, grad_near, grad_far)
    return outs[:planes], outs[planes:]


def project(pieces, out_weight, chips, width):
    row_count = pieces[0].shape[0]
    out_width = out_weight.shape[1]

    def kernel(*refs):
        ins, weight, out = refs[:chips], refs[chips], refs[chips + 1]
        chip, _ = place()
        step = min(out_width, 512)
        for column in range(0, out_width, step):
            value = None
            for away in range(chips):
                start = pl.multiple_of((chip ^ away) * width, width)
                part = jnp.dot(
                    ins[away][...],
                    weight[pl.ds(start, width), column : column + step],
                    preferred_element_type=jnp.float32,
                )
                value = part if value is None else value + part
            out[:, column : column + step] = value.astype(out.dtype)

    return pl.pallas_call(
        kernel,
        out_shape=jax.ShapeDtypeStruct((row_count, out_width), jnp.bfloat16),
        in_specs=[VMEM] * (chips + 1),
        out_specs=VMEM,
        compiler_params=params(24),
        cost_estimate=pl.CostEstimate(
            flops=2 * row_count * out_weight.size,
            bytes_accessed=2 * out_weight.size,
            transcendentals=0,
        ),
        name="project",
    )(*pieces, out_weight)


def add_up(own, others, axis, size):
    group = own.shape[0] // size

    def kernel(*refs):
        ins, outs = refs[: 1 + len(others)], refs[1 + len(others) :]
        here = lax.axis_index("dp") if axis == "dp" else place()[0]
        for away in range(size):
            rows = pl.ds(pl.multiple_of((here ^ away) * group, group), group)
            value = ins[0][rows, :]
            for ref in ins[1:]:
                value = value + ref[rows, :].astype(jnp.float32)
            outs[away][...] = value.astype(outs[away].dtype)

    return pl.pallas_call(
        kernel,
        out_shape=[
            jax.ShapeDtypeStruct(
                (group, own.shape[1]), jnp.float32 if away == 0 else jnp.bfloat16
            )
            for away in range(size)
        ],
        in_specs=[VMEM] * (1 + len(others)),
        out_specs=[VMEM] * size,
        compiler_params=params(16),
        name="add_up",
    )(own, *others)


def finish(lefts, rights):
    rows, split = lefts[0].shape
    width = split + rights[0].shape[1]

    def kernel(*refs):
        ins, out = refs[:-1], refs[-1]
        for group, columns in (
            (ins[: len(lefts)], slice(0, split)),
            (ins[len(lefts) :], slice(split, width)),
        ):
            value = group[0][...]
            for ref in group[1:]:
                value = value + ref[...].astype(jnp.float32)
            out[:, columns] = value

    return pl.pallas_call(
        kernel,
        out_shape=jax.ShapeDtypeStruct((rows, width), jnp.float32),
        in_specs=[VMEM] * (len(lefts) + len(rights)),
        out_specs=VMEM,
        compiler_params=params(16),
        name="finish",
    )(*lefts, *rights)


def body(seq, planes, query_rows, key_rows, value_rows, scale_end, out_weight, grad_out):
    chips = seq // 2
    full = query_rows.shape[2]
    width = full // chips

    def over(axis, size, value, mask):
        return lax.ppermute(value, axis, [(i, i ^ mask) for i in range(size)])

    def other_core(value):
        return over("seq", seq, value, 1)

    def spread(pieces):
        return [pieces[0]] + [over("seq", seq, pieces[away], 2 * away) for away in range(1, chips)]

    def meet(pieces):
        return [pieces[0]] + [over("dp", planes, pieces[away], away) for away in range(1, planes)]

    near = spread(cut([key_rows[0], value_rows[0]], chips, width))
    queries = spread(cut([query_rows[0]], chips, width))
    ends = spread([scale_end] * chips)
    far = [other_core(piece) for piece in near]
    grad_near = grad_out[0]
    grad_far = other_core(grad_near)
    both = assemble(near, far, chips)
    mine = [None] * chips
    for aways in (list(range(chips - 1)), [chips - 1]):
        results = attend([queries[i] for i in aways], [ends[i] for i in aways], aways, both, width)
        for away, piece in zip(aways, results):
            mine[away] = over("seq", seq, piece, 2 * away) if away else piece
    others = [other_core(piece) for piece in mine]
    out_width = out_weight.shape[1]
    split = out_width * 5 // 8
    by_plane, by_chip = weight_gradient(
        mine, others, grad_near, grad_far, chips, width, planes, split
    )
    met = meet(by_plane)
    gathered = spread(by_chip)
    mixed_out = project(mine, out_weight, chips, width)[None]
    lefts = meet(add_up(gathered[0], gathered[1:], "dp", planes))
    rights = spread(add_up(met[0], met[1:], "seq", chips))
    return mixed_out, finish(lefts, rights)


def solution(mesh):
    placed = (
        P("dp", "seq", None),
        P("dp", "seq", None),
        P("dp", "seq", None),
        P("seq"),
        P(),
        P("dp", "seq", None),
    )
    seq, planes = mesh.shape["seq"], mesh.shape["dp"]
    return jax.shard_map(
        functools.partial(body, seq, planes),
        mesh=mesh,
        in_specs=placed,
        out_specs=(P("dp", "seq", None), P(("dp", "seq"), None)),
        check_vma=False,
    )
```

```python
import functools

import jax
import jax.numpy as jnp
from jax import lax
from jax.experimental import pallas as pl
from jax.experimental.pallas import tpu as pltpu
from jax.sharding import PartitionSpec as P


HEAD = 128
FLOOR = -1e30
SCALES = 4
LOG2E = 1.4426950408889634


HBM = pl.BlockSpec(memory_space=pltpu.HBM)
VMEM = pl.BlockSpec(memory_space=pltpu.VMEM)
SMEM = pl.BlockSpec(memory_space=pltpu.SMEM)


def place():
    index = lax.axis_index("seq")
    return index // 2, index % 2


def params(mebibytes):
    return pltpu.CompilerParams(vmem_limit_bytes=mebibytes * 1024 * 1024)


def cut(sources, chips, width):
    row_count = sources[0].shape[0]
    count = len(sources)

    def kernel(*refs):
        ins, outs, sems = refs[:count], refs[count:-1], refs[-1]
        chip, _ = place()
        copies = []
        for away in reversed(range(chips)):
            columns = pl.ds(pl.multiple_of((chip ^ away) * width, width), width)
            for at, source in enumerate(ins):
                copies.append(
                    pltpu.make_async_copy(
                        source.at[:, columns],
                        outs[away].at[:, at * width : (at + 1) * width],
                        sems.at[len(copies)],
                    )
                )
        for copy in copies:
            copy.start()
        for copy in copies:
            copy.wait()

    shape = jax.ShapeDtypeStruct((row_count, count * width), sources[0].dtype)
    return pl.pallas_call(
        kernel,
        out_shape=[shape] * chips,
        in_specs=[HBM] * count,
        out_specs=[VMEM] * chips,
        scratch_shapes=[pltpu.SemaphoreType.DMA((count * chips,))],
        compiler_params=params(16),
        name="cut",
    )(*(pltpu.with_memory_space_constraint(source, pltpu.HBM) for source in sources))


def assemble(near, far, chips):
    row_count, wide = near[0].shape

    def kernel(*refs):
        pieces, out = (refs[:chips], refs[chips : 2 * chips]), refs[2 * chips]
        chip, core = place()
        for away in range(chips):
            for side in range(2):
                at = (chip ^ away) * 2 + (core ^ side)
                rows = pl.ds(pl.multiple_of(at * row_count, row_count), row_count)
                out[rows, :] = pieces[side][away][...]

    return pl.pallas_call(
        kernel,
        out_shape=jax.ShapeDtypeStruct((2 * chips * row_count, wide), near[0].dtype),
        in_specs=[VMEM] * (2 * chips),
        out_specs=VMEM,
        compiler_params=params(16),
        name="assemble",
    )(*near, *far)


def attend(queries, ends, aways, both, width):
    row_count = queries[0].shape[0]
    total = both.shape[0]
    heads = width // HEAD
    count = len(queries)
    choices = 3
    step_k = total // choices
    scale = float(HEAD) ** -0.5 * LOG2E

    def kernel(*refs):
        ends_in = refs[:count]
        q_in = refs[count : 2 * count]
        both_ref = refs[2 * count]
        outs = refs[2 * count + 1 : 3 * count + 1]
        qbuf, obuf, sbuf = refs[3 * count + 1 :]
        chip, core = place()

        def block(index, starts, limits, steps):
            token = starts + lax.broadcasted_iota(jnp.int32, (row_count, HEAD), 0)
            limit = jnp.full((row_count, HEAD), limits[-1], jnp.int32)
            for value in reversed(limits[:-1]):
                limit = jnp.where(token < value, value, limit)
            room = limit - lax.broadcasted_iota(jnp.int32, (row_count, HEAD), 1)
            shifts = []
            for head in range(heads):
                columns = slice(head * HEAD, (head + 1) * HEAD)
                query = qbuf[index, :, columns]
                top = None
                for at in range(0, steps * step_k, step_k):
                    score = lax.dot_general(
                        query,
                        both_ref[at : at + step_k, columns],
                        (((1,), (1,)), ((), ())),
                        preferred_element_type=jnp.float32,
                    )
                    for base in range(0, step_k, HEAD):
                        part = jnp.where(room > at + base, score[:, base : base + HEAD], FLOOR)
                        sbuf[head, :, at + base : at + base + HEAD] = part
                        top = part if top is None else jnp.maximum(top, part)
                shifts.append(jnp.max(top, axis=1, keepdims=True) * scale)
            for head in range(heads):
                columns = slice(head * HEAD, (head + 1) * HEAD)
                tally = acc = None
                for at in range(0, steps * step_k, step_k):
                    weights = jnp.exp2(sbuf[head, :, at : at + step_k] * scale - shifts[head])
                    for base in range(0, step_k, HEAD):
                        part = weights[:, base : base + HEAD]
                        tally = part if tally is None else tally + part
                    product = jnp.dot(
                        weights.astype(jnp.bfloat16),
                        both_ref[at : at + step_k, width + head * HEAD : width + (head + 1) * HEAD],
                        preferred_element_type=jnp.float32,
                    )
                    acc = product if acc is None else acc + product
                obuf[index, :, columns] = (acc / jnp.sum(tally, axis=1, keepdims=True)).astype(
                    obuf.dtype
                )

        starts, limits = [], []
        for index, away in enumerate(aways):
            qbuf[index] = q_in[index][...]
            start = ((chip ^ away) * 2 + core) * row_count
            limit = [ends_in[index][0]]
            for _ in range(SCALES - 1):
                limit.append(ends_in[index][jnp.minimum(limit[-1] - start, row_count - 1)])
            starts.append(start)
            limits.append(limit)

        def turn(index, carry):
            def pick(values):
                value = values[0]
                for at in range(1, count):
                    value = jnp.where(index == at, values[at], value)
                return value

            start = pick(starts)
            limit = [pick([one[at] for one in limits]) for at in range(SCALES)]
            needed = (limit[-1] + step_k - 1) // step_k
            for steps in range(1, choices + 1):

                @pl.when(needed == steps)
                def _(steps=steps):
                    block(index, start, limit, steps)

            return carry

        lax.fori_loop(0, count, turn, 0)
        for index in range(count):
            outs[index][...] = obuf[index]

    return pl.pallas_call(
        kernel,
        out_shape=[jax.ShapeDtypeStruct((row_count, width), jnp.bfloat16)] * count,
        in_specs=[SMEM] * count + [VMEM] * (count + 1),
        out_specs=[VMEM] * count,
        scratch_shapes=[
            pltpu.VMEM((count, row_count, width), jnp.bfloat16),
            pltpu.VMEM((count, row_count, width), jnp.bfloat16),
            pltpu.VMEM((heads, row_count, total), jnp.float32),
        ],
        compiler_params=params(30),
        cost_estimate=pl.CostEstimate(
            flops=4 * count * row_count * total * width,
            bytes_accessed=4 * total * width,
            transcendentals=count * row_count * total * heads,
        ),
        name="attend",
    )(*ends, *queries, both)


def weight_gradient(near, far, grad_near, grad_far, chips, width, planes, split):
    row_count = near[0].shape[0]
    full = chips * width
    out_width = grad_near.shape[1]
    group = full // (planes * chips * 2)

    def kernel(*refs):
        pieces = (refs[0:chips], refs[chips : 2 * chips])
        grads = refs[2 * chips : 2 * chips + 2]
        by_plane = refs[2 * chips + 2 : 2 * chips + 2 + planes]
        by_chip = refs[2 * chips + 2 + planes : 3 * chips + 2 + planes]
        turned, left = refs[3 * chips + 2 + planes :]
        chip, core = place()
        here = lax.axis_index("dp")
        for side in range(2):
            for away in range(chips):
                start = pl.multiple_of((chip ^ away) * width, width)
                turned[pl.ds(start, width), side * row_count : (side + 1) * row_count] = (
                    pieces[side][away][...].T
                )

        def product(outs, columns, picks):
            for out, starts in zip(outs, picks):
                for at, start in enumerate(starts):
                    rows = pl.ds(pl.multiple_of((start * 2 + core) * group, group), group)
                    left[at * group : (at + 1) * group, :] = turned[rows, :]
                size = len(starts) * group
                value = jnp.dot(
                    left[:size, :row_count], grads[0][:, columns], preferred_element_type=jnp.float32
                ) + jnp.dot(
                    left[:size, row_count:], grads[1][:, columns], preferred_element_type=jnp.float32
                )
                out[...] = value.astype(out.dtype)

        product(
            by_plane,
            slice(split, out_width),
            [[(here ^ far_) * chips + at for at in range(chips)] for far_ in range(planes)],
        )
        product(
            by_chip,
            slice(0, split),
            [[at * chips + (chip ^ far_) for at in range(planes)] for far_ in range(chips)],
        )

    def shape(rows, columns, away):
        return jax.ShapeDtypeStruct((rows, columns), jnp.float32 if away == 0 else jnp.bfloat16)

    outs = pl.pallas_call(
        kernel,
        out_shape=[shape(chips * group, out_width - split, away) for away in range(planes)]
        + [shape(planes * group, split, away) for away in range(chips)],
        in_specs=[VMEM] * (2 * chips + 2),
        out_specs=[VMEM] * (planes + chips),
        scratch_shapes=[
            pltpu.VMEM((full, 2 * row_count), jnp.bfloat16),
            pltpu.VMEM((max(planes, chips) * group, 2 * row_count), jnp.bfloat16),
        ],
        compiler_params=params(32),
        cost_estimate=pl.CostEstimate(
            flops=2 * full * row_count * out_width,
            bytes_accessed=4 * row_count * out_width,
            transcendentals=0,
        ),
        name="weight_gradient",
    )(*near, *far, grad_near, grad_far)
    return outs[:planes], outs[planes:]


def project(pieces, out_weight, chips, width):
    row_count = pieces[0].shape[0]
    out_width = out_weight.shape[1]

    def kernel(*refs):
        ins, weight, out = refs[:chips], refs[chips], refs[chips + 1]
        chip, _ = place()
        step = min(out_width, 512)
        for column in range(0, out_width, step):
            value = None
            for away in range(chips):
                start = pl.multiple_of((chip ^ away) * width, width)
                part = jnp.dot(
                    ins[away][...],
                    weight[pl.ds(start, width), column : column + step],
                    preferred_element_type=jnp.float32,
                )
                value = part if value is None else value + part
            out[:, column : column + step] = value.astype(out.dtype)

    return pl.pallas_call(
        kernel,
        out_shape=jax.ShapeDtypeStruct((row_count, out_width), jnp.bfloat16),
        in_specs=[VMEM] * (chips + 1),
        out_specs=VMEM,
        compiler_params=params(24),
        cost_estimate=pl.CostEstimate(
            flops=2 * row_count * out_weight.size,
            bytes_accessed=2 * out_weight.size,
            transcendentals=0,
        ),
        name="project",
    )(*pieces, out_weight)


def add_up(own, others, axis, size):
    group = own.shape[0] // size

    def kernel(*refs):
        ins, outs = refs[: 1 + len(others)], refs[1 + len(others) :]
        here = lax.axis_index("dp") if axis == "dp" else place()[0]
        for away in range(size):
            rows = pl.ds(pl.multiple_of((here ^ away) * group, group), group)
            value = ins[0][rows, :]
            for ref in ins[1:]:
                value = value + ref[rows, :].astype(jnp.float32)
            outs[away][...] = value.astype(outs[away].dtype)

    return pl.pallas_call(
        kernel,
        out_shape=[
            jax.ShapeDtypeStruct(
                (group, own.shape[1]), jnp.float32 if away == 0 else jnp.bfloat16
            )
            for away in range(size)
        ],
        in_specs=[VMEM] * (1 + len(others)),
        out_specs=[VMEM] * size,
        compiler_params=params(16),
        name="add_up",
    )(own, *others)


def finish(lefts, rights):
    rows, split = lefts[0].shape
    width = split + rights[0].shape[1]

    def kernel(*refs):
        ins, out = refs[:-1], refs[-1]
        for group, columns in (
            (ins[: len(lefts)], slice(0, split)),
            (ins[len(lefts) :], slice(split, width)),
        ):
            value = group[0][...]
            for ref in group[1:]:
                value = value + ref[...].astype(jnp.float32)
            out[:, columns] = value

    return pl.pallas_call(
        kernel,
        out_shape=jax.ShapeDtypeStruct((rows, width), jnp.float32),
        in_specs=[VMEM] * (len(lefts) + len(rights)),
        out_specs=VMEM,
        compiler_params=params(16),
        name="finish",
    )(*lefts, *rights)


def body(seq, planes, query_rows, key_rows, value_rows, scale_end, out_weight, grad_out):
    chips = seq // 2
    full = query_rows.shape[2]
    width = full // chips

    def over(axis, size, value, mask):
        return lax.ppermute(value, axis, [(i, i ^ mask) for i in range(size)])

    def other_core(value):
        return over("seq", seq, value, 1)

    def spread(pieces):
        return [pieces[0]] + [over("seq", seq, pieces[away], 2 * away) for away in range(1, chips)]

    def meet(pieces):
        return [pieces[0]] + [over("dp", planes, pieces[away], away) for away in range(1, planes)]

    near = spread(cut([key_rows[0], value_rows[0]], chips, width))
    queries = spread(cut([query_rows[0]], chips, width))
    ends = spread([scale_end] * chips)
    far = [other_core(piece) for piece in near]
    grad_near = grad_out[0]
    grad_far = other_core(grad_near)
    both = assemble(near, far, chips)
    mine = [None] * chips
    for aways in ([chips - 1], list(range(1, chips - 1)), [0]):
        results = attend([queries[i] for i in aways], [ends[i] for i in aways], aways, both, width)
        for away, piece in zip(aways, results):
            mine[away] = over("seq", seq, piece, 2 * away) if away else piece
    others = [other_core(piece) for piece in mine]
    out_width = out_weight.shape[1]
    split = out_width * 5 // 8
    by_plane, by_chip = weight_gradient(
        mine, others, grad_near, grad_far, chips, width, planes, split
    )
    met = meet(by_plane)
    gathered = spread(by_chip)
    mixed_out = project(mine, out_weight, chips, width)[None]
    lefts = meet(add_up(gathered[0], gathered[1:], "dp", planes))
    rights = spread(add_up(met[0], met[1:], "seq", chips))
    return mixed_out, finish(lefts, rights)


def solution(mesh):
    placed = (
        P("dp", "seq", None),
        P("dp", "seq", None),
        P("dp", "seq", None),
        P("seq"),
        P(),
        P("dp", "seq", None),
    )
    seq, planes = mesh.shape["seq"], mesh.shape["dp"]
    return jax.shard_map(
        functools.partial(body, seq, planes),
        mesh=mesh,
        in_specs=placed,
        out_specs=(P("dp", "seq", None), P(("dp", "seq"), None)),
        check_vma=False,
    )
```

```python
import functools

import jax
import jax.numpy as jnp
from jax import lax
from jax.experimental import pallas as pl
from jax.experimental.pallas import tpu as pltpu
from jax.sharding import PartitionSpec as P


HEAD = 128
FLOOR = -1e30
SCALES = 4
LOG2E = 1.4426950408889634


HBM = pl.BlockSpec(memory_space=pltpu.HBM)
VMEM = pl.BlockSpec(memory_space=pltpu.VMEM)
SMEM = pl.BlockSpec(memory_space=pltpu.SMEM)


def place():
    index = lax.axis_index("seq")
    return index // 2, index % 2


def params(mebibytes):
    return pltpu.CompilerParams(vmem_limit_bytes=mebibytes * 1024 * 1024)


def cut(sources, chips, width):
    row_count = sources[0].shape[0]
    count = len(sources)

    def kernel(*refs):
        ins, outs, sems = refs[:count], refs[count:-1], refs[-1]
        chip, _ = place()
        copies = []
        for away in reversed(range(chips)):
            columns = pl.ds(pl.multiple_of((chip ^ away) * width, width), width)
            for at, source in enumerate(ins):
                copies.append(
                    pltpu.make_async_copy(
                        source.at[:, columns],
                        outs[away].at[:, at * width : (at + 1) * width],
                        sems.at[len(copies)],
                    )
                )
        for copy in copies:
            copy.start()
        for copy in copies:
            copy.wait()

    shape = jax.ShapeDtypeStruct((row_count, count * width), sources[0].dtype)
    return pl.pallas_call(
        kernel,
        out_shape=[shape] * chips,
        in_specs=[HBM] * count,
        out_specs=[VMEM] * chips,
        scratch_shapes=[pltpu.SemaphoreType.DMA((count * chips,))],
        compiler_params=params(16),
        name="cut",
    )(*(pltpu.with_memory_space_constraint(source, pltpu.HBM) for source in sources))


def assemble(near, far, chips):
    row_count, wide = near[0].shape

    def kernel(*refs):
        pieces, out = (refs[:chips], refs[chips : 2 * chips]), refs[2 * chips]
        chip, core = place()
        for away in range(chips):
            for side in range(2):
                at = (chip ^ away) * 2 + (core ^ side)
                rows = pl.ds(pl.multiple_of(at * row_count, row_count), row_count)
                out[rows, :] = pieces[side][away][...]

    return pl.pallas_call(
        kernel,
        out_shape=jax.ShapeDtypeStruct((2 * chips * row_count, wide), near[0].dtype),
        in_specs=[VMEM] * (2 * chips),
        out_specs=VMEM,
        compiler_params=params(16),
        name="assemble",
    )(*near, *far)


def attend(queries, ends, aways, both, width):
    row_count = queries[0].shape[0]
    total = both.shape[0]
    heads = width // HEAD
    count = len(queries)
    step_k = total // 4
    scale = float(HEAD) ** -0.5 * LOG2E

    def kernel(*refs):
        ends_in = refs[:count]
        q_in = refs[count : 2 * count]
        both_ref = refs[2 * count]
        outs = refs[2 * count + 1 : 3 * count + 1]
        qbuf, obuf, sbuf, sums, tallies, tops = refs[3 * count + 1 :]
        chip, core = place()

        def part(index, room, base, steps):
            shifts, factors = [], []
            for head in range(heads):
                columns = slice(head * HEAD, (head + 1) * HEAD)
                query = qbuf[index, :, columns]
                top = None
                for at in range(base, base + steps * step_k, step_k):
                    score = lax.dot_general(
                        query,
                        both_ref[at : at + step_k, columns],
                        (((1,), (1,)), ((), ())),
                        preferred_element_type=jnp.float32,
                    )
                    for key in range(0, step_k, HEAD):
                        piece = jnp.where(room > at + key, score[:, key : key + HEAD], FLOOR)
                        sbuf[head, :, at - base + key : at - base + key + HEAD] = piece
                        top = piece if top is None else jnp.maximum(top, piece)
                shift = jnp.broadcast_to(jnp.max(top, axis=1, keepdims=True), top.shape) * scale
                if base:
                    before = tops[head]
                    shift = jnp.maximum(before, shift)
                    factors.append(jnp.exp2(before - shift))
                shifts.append(shift)
            for head in range(heads):
                tally = acc = None
                for at in range(base, base + steps * step_k, step_k):
                    weights = []
                    for key in range(0, step_k, HEAD):
                        piece = sbuf[head, :, at - base + key : at - base + key + HEAD]
                        piece = jnp.exp2(piece * scale - shifts[head])
                        tally = piece if tally is None else tally + piece
                        weights.append(piece.astype(jnp.bfloat16))
                    product = jnp.dot(
                        jnp.concatenate(weights, axis=1),
                        both_ref[at : at + step_k, width + head * HEAD : width + (head + 1) * HEAD],
                        preferred_element_type=jnp.float32,
                    )
                    acc = product if acc is None else acc + product
                if base:
                    acc = acc + sums[head] * factors[head]
                    tally = tally + tallies[head] * factors[head]
                sums[head], tallies[head], tops[head] = acc, tally, shifts[head]

        starts, limits = [], []
        for index, away in enumerate(aways):
            qbuf[index] = q_in[index][...]
            start = ((chip ^ away) * 2 + core) * row_count
            limit = [ends_in[index][0]]
            for _ in range(SCALES - 1):
                limit.append(ends_in[index][jnp.minimum(limit[-1] - start, row_count - 1)])
            starts.append(start)
            limits.append(limit)

        def turn(index, carry):
            def pick(values):
                value = values[0]
                for at in range(1, count):
                    value = jnp.where(index == at, values[at], value)
                return value

            limit = [pick([one[at] for one in limits]) for at in range(SCALES)]
            needed = (limit[-1] + step_k - 1) // step_k
            token = pick(starts) + lax.broadcasted_iota(jnp.int32, (row_count, HEAD), 0)
            bound = jnp.full((row_count, HEAD), limit[-1], jnp.int32)
            for value in reversed(limit[:-1]):
                bound = jnp.where(token < value, value, bound)
            room = bound - lax.broadcasted_iota(jnp.int32, (row_count, HEAD), 1)
            for test, base, steps in (
                (needed == 1, 0, 1),
                (needed >= 2, 0, 2),
                (needed == 3, 2 * step_k, 1),
                (needed == 4, 2 * step_k, 2),
            ):

                @pl.when(test)
                def _(base=base, steps=steps):
                    part(index, room, base, steps)

            for head in range(heads):
                obuf[index, :, head * HEAD : (head + 1) * HEAD] = (
                    sums[head] / jnp.sum(tallies[head], axis=1, keepdims=True)
                ).astype(obuf.dtype)
            return carry

        lax.fori_loop(0, count, turn, 0)
        for index in range(count):
            outs[index][...] = obuf[index]

    state = pltpu.VMEM((heads, row_count, HEAD), jnp.float32)
    return pl.pallas_call(
        kernel,
        out_shape=[jax.ShapeDtypeStruct((row_count, width), jnp.bfloat16)] * count,
        in_specs=[SMEM] * count + [VMEM] * (count + 1),
        out_specs=[VMEM] * count,
        scratch_shapes=[
            pltpu.VMEM((count, row_count, width), jnp.bfloat16),
            pltpu.VMEM((count, row_count, width), jnp.bfloat16),
            pltpu.VMEM((heads, row_count, total // 2), jnp.float32),
            state,
            state,
            state,
        ],
        compiler_params=params(30),
        cost_estimate=pl.CostEstimate(
            flops=4 * count * row_count * total * width,
            bytes_accessed=4 * total * width,
            transcendentals=count * row_count * total * heads,
        ),
        name="attend",
    )(*ends, *queries, both)


def weight_gradient(near, far, grad_near, grad_far, chips, width, planes, split):
    row_count = near[0].shape[0]
    full = chips * width
    out_width = grad_near.shape[1]
    group = full // (planes * chips * 2)

    def kernel(*refs):
        pieces = (refs[0:chips], refs[chips : 2 * chips])
        grads = refs[2 * chips : 2 * chips + 2]
        by_plane = refs[2 * chips + 2 : 2 * chips + 2 + planes]
        by_chip = refs[2 * chips + 2 + planes : 3 * chips + 2 + planes]
        turned, left = refs[3 * chips + 2 + planes :]
        chip, core = place()
        here = lax.axis_index("dp")
        for side in range(2):
            for away in range(chips):
                start = pl.multiple_of((chip ^ away) * width, width)
                turned[pl.ds(start, width), side * row_count : (side + 1) * row_count] = (
                    pieces[side][away][...].T
                )

        def product(outs, columns, picks):
            for out, starts in zip(outs, picks):
                for at, start in enumerate(starts):
                    rows = pl.ds(pl.multiple_of((start * 2 + core) * group, group), group)
                    left[at * group : (at + 1) * group, :] = turned[rows, :]
                size = len(starts) * group
                value = jnp.dot(
                    left[:size, :row_count], grads[0][:, columns], preferred_element_type=jnp.float32
                ) + jnp.dot(
                    left[:size, row_count:], grads[1][:, columns], preferred_element_type=jnp.float32
                )
                out[...] = value.astype(out.dtype)

        product(
            by_plane,
            slice(split, out_width),
            [[(here ^ far_) * chips + at for at in range(chips)] for far_ in range(planes)],
        )
        product(
            by_chip,
            slice(0, split),
            [[at * chips + (chip ^ far_) for at in range(planes)] for far_ in range(chips)],
        )

    def shape(rows, columns, away):
        return jax.ShapeDtypeStruct((rows, columns), jnp.float32 if away == 0 else jnp.bfloat16)

    outs = pl.pallas_call(
        kernel,
        out_shape=[shape(chips * group, out_width - split, away) for away in range(planes)]
        + [shape(planes * group, split, away) for away in range(chips)],
        in_specs=[VMEM] * (2 * chips + 2),
        out_specs=[VMEM] * (planes + chips),
        scratch_shapes=[
            pltpu.VMEM((full, 2 * row_count), jnp.bfloat16),
            pltpu.VMEM((max(planes, chips) * group, 2 * row_count), jnp.bfloat16),
        ],
        compiler_params=params(32),
        cost_estimate=pl.CostEstimate(
            flops=2 * full * row_count * out_width,
            bytes_accessed=4 * row_count * out_width,
            transcendentals=0,
        ),
        name="weight_gradient",
    )(*near, *far, grad_near, grad_far)
    return outs[:planes], outs[planes:]


def project(pieces, out_weight, chips, width):
    row_count = pieces[0].shape[0]
    out_width = out_weight.shape[1]

    def kernel(*refs):
        ins, weight, out = refs[:chips], refs[chips], refs[chips + 1]
        chip, _ = place()
        step = min(out_width, 512)
        for column in range(0, out_width, step):
            value = None
            for away in range(chips):
                start = pl.multiple_of((chip ^ away) * width, width)
                part = jnp.dot(
                    ins[away][...],
                    weight[pl.ds(start, width), column : column + step],
                    preferred_element_type=jnp.float32,
                )
                value = part if value is None else value + part
            out[:, column : column + step] = value.astype(out.dtype)

    return pl.pallas_call(
        kernel,
        out_shape=jax.ShapeDtypeStruct((row_count, out_width), jnp.bfloat16),
        in_specs=[VMEM] * (chips + 1),
        out_specs=VMEM,
        compiler_params=params(24),
        cost_estimate=pl.CostEstimate(
            flops=2 * row_count * out_weight.size,
            bytes_accessed=2 * out_weight.size,
            transcendentals=0,
        ),
        name="project",
    )(*pieces, out_weight)


def add_up(own, others, axis, size):
    group = own.shape[0] // size

    def kernel(*refs):
        ins, outs = refs[: 1 + len(others)], refs[1 + len(others) :]
        here = lax.axis_index("dp") if axis == "dp" else place()[0]
        for away in range(size):
            rows = pl.ds(pl.multiple_of((here ^ away) * group, group), group)
            value = ins[0][rows, :]
            for ref in ins[1:]:
                value = value + ref[rows, :].astype(jnp.float32)
            outs[away][...] = value.astype(outs[away].dtype)

    return pl.pallas_call(
        kernel,
        out_shape=[
            jax.ShapeDtypeStruct(
                (group, own.shape[1]), jnp.float32 if away == 0 else jnp.bfloat16
            )
            for away in range(size)
        ],
        in_specs=[VMEM] * (1 + len(others)),
        out_specs=[VMEM] * size,
        compiler_params=params(16),
        name="add_up",
    )(own, *others)


def finish(lefts, rights):
    rows, split = lefts[0].shape
    width = split + rights[0].shape[1]

    def kernel(*refs):
        ins, out = refs[:-1], refs[-1]
        for group, columns in (
            (ins[: len(lefts)], slice(0, split)),
            (ins[len(lefts) :], slice(split, width)),
        ):
            value = group[0][...]
            for ref in group[1:]:
                value = value + ref[...].astype(jnp.float32)
            out[:, columns] = value

    return pl.pallas_call(
        kernel,
        out_shape=jax.ShapeDtypeStruct((rows, width), jnp.float32),
        in_specs=[VMEM] * (len(lefts) + len(rights)),
        out_specs=VMEM,
        compiler_params=params(16),
        name="finish",
    )(*lefts, *rights)


def body(seq, planes, query_rows, key_rows, value_rows, scale_end, out_weight, grad_out):
    chips = seq // 2
    full = query_rows.shape[2]
    width = full // chips

    def over(axis, size, value, mask):
        return lax.ppermute(value, axis, [(i, i ^ mask) for i in range(size)])

    def other_core(value):
        return over("seq", seq, value, 1)

    def spread(pieces):
        return [pieces[0]] + [over("seq", seq, pieces[away], 2 * away) for away in range(1, chips)]

    def meet(pieces):
        return [pieces[0]] + [over("dp", planes, pieces[away], away) for away in range(1, planes)]

    near = spread(cut([key_rows[0], value_rows[0]], chips, width))
    queries = spread(cut([query_rows[0]], chips, width))
    ends = spread([scale_end] * chips)
    far = [other_core(piece) for piece in near]
    grad_near = grad_out[0]
    grad_far = other_core(grad_near)
    both = assemble(near, far, chips)
    mine = [None] * chips
    for aways in ([chips - 1], list(range(1, chips - 1)), [0]):
        results = attend(
            [queries[i] for i in aways], [ends[i] for i in aways], aways, both, width
        )
        for away, piece in zip(aways, results):
            mine[away] = over("seq", seq, piece, 2 * away) if away else piece
    others = [other_core(piece) for piece in mine]
    out_width = out_weight.shape[1]
    split = out_width * 11 // 16
    by_plane, by_chip = weight_gradient(
        mine, others, grad_near, grad_far, chips, width, planes, split
    )
    met = meet(by_plane)
    gathered = spread(by_chip)
    mixed_out = project(mine, out_weight, chips, width)[None]
    lefts = meet(add_up(gathered[0], gathered[1:], "dp", planes))
    rights = spread(add_up(met[0], met[1:], "seq", chips))
    return mixed_out, finish(lefts, rights)


def solution(mesh):
    placed = (
        P("dp", "seq", None),
        P("dp", "seq", None),
        P("dp", "seq", None),
        P("seq"),
        P(),
        P("dp", "seq", None),
    )
    seq, planes = mesh.shape["seq"], mesh.shape["dp"]
    return jax.shard_map(
        functools.partial(body, seq, planes),
        mesh=mesh,
        in_specs=placed,
        out_specs=(P("dp", "seq", None), P(("dp", "seq"), None)),
        check_vma=False,
    )
```

```python
import functools

import jax
import jax.numpy as jnp
from jax import lax
from jax.experimental import pallas as pl
from jax.experimental.pallas import tpu as pltpu
from jax.sharding import PartitionSpec as P


HEAD = 128
FLOOR = -1e30
SCALES = 4
LOG2E = 1.4426950408889634


HBM = pl.BlockSpec(memory_space=pltpu.HBM)
VMEM = pl.BlockSpec(memory_space=pltpu.VMEM)
SMEM = pl.BlockSpec(memory_space=pltpu.SMEM)


def place():
    index = lax.axis_index("seq")
    return index // 2, index % 2


def params(mebibytes):
    return pltpu.CompilerParams(vmem_limit_bytes=mebibytes * 1024 * 1024)


def cut(sources, aways, width):
    row_count = sources[0].shape[0]
    count = len(sources)

    def kernel(*refs):
        ins, outs, sems = refs[:count], refs[count:-1], refs[-1]
        chip, _ = place()
        copies = []
        for out, away in zip(outs, aways):
            columns = pl.ds(pl.multiple_of((chip ^ away) * width, width), width)
            for at, source in enumerate(ins):
                copies.append(
                    pltpu.make_async_copy(
                        source.at[:, columns],
                        out.at[:, at * width : (at + 1) * width],
                        sems.at[len(copies)],
                    )
                )
        for copy in copies:
            copy.start()
        for copy in copies:
            copy.wait()

    shape = jax.ShapeDtypeStruct((row_count, count * width), sources[0].dtype)
    return pl.pallas_call(
        kernel,
        out_shape=[shape] * len(aways),
        in_specs=[HBM] * count,
        out_specs=[VMEM] * len(aways),
        scratch_shapes=[pltpu.SemaphoreType.DMA((count * len(aways),))],
        compiler_params=params(16),
        name="cut",
    )(*(pltpu.with_memory_space_constraint(source, pltpu.HBM) for source in sources))


def assemble(near, far, chips):
    row_count, wide = near[0].shape

    def kernel(*refs):
        pieces, out = (refs[:chips], refs[chips : 2 * chips]), refs[2 * chips]
        chip, core = place()
        for away in range(chips):
            for side in range(2):
                at = (chip ^ away) * 2 + (core ^ side)
                rows = pl.ds(pl.multiple_of(at * row_count, row_count), row_count)
                out[rows, :] = pieces[side][away][...]

    return pl.pallas_call(
        kernel,
        out_shape=jax.ShapeDtypeStruct((2 * chips * row_count, wide), near[0].dtype),
        in_specs=[VMEM] * (2 * chips),
        out_specs=VMEM,
        compiler_params=params(16),
        name="assemble",
    )(*near, *far)


def attend(queries, ends, aways, both, width):
    row_count = queries[0].shape[0]
    total = both.shape[0]
    heads = width // HEAD
    count = len(queries)
    step_k = total // 4
    scale = float(HEAD) ** -0.5 * LOG2E

    def kernel(*refs):
        ends_in = refs[:count]
        q_in = refs[count : 2 * count]
        both_ref = refs[2 * count]
        outs = refs[2 * count + 1 : 3 * count + 1]
        qbuf, obuf, sbuf, sums, tallies, tops = refs[3 * count + 1 :]
        chip, core = place()

        def part(index, room, base, steps):
            shifts, factors = [], []
            for head in range(heads):
                columns = slice(head * HEAD, (head + 1) * HEAD)
                query = qbuf[index, :, columns]
                top = None
                for at in range(base, base + steps * step_k, step_k):
                    score = lax.dot_general(
                        query,
                        both_ref[at : at + step_k, columns],
                        (((1,), (1,)), ((), ())),
                        preferred_element_type=jnp.float32,
                    )
                    for key in range(0, step_k, HEAD):
                        piece = jnp.where(room > at + key, score[:, key : key + HEAD], FLOOR)
                        sbuf[head, :, at - base + key : at - base + key + HEAD] = piece
                        top = piece if top is None else jnp.maximum(top, piece)
                shift = jnp.broadcast_to(jnp.max(top, axis=1, keepdims=True), top.shape) * scale
                if base:
                    before = tops[head]
                    shift = jnp.maximum(before, shift)
                    factors.append(jnp.exp2(before - shift))
                shifts.append(shift)
            for head in range(heads):
                tally = acc = None
                for at in range(base, base + steps * step_k, step_k):
                    weights = []
                    for key in range(0, step_k, HEAD):
                        piece = sbuf[head, :, at - base + key : at - base + key + HEAD]
                        piece = jnp.exp2(piece * scale - shifts[head])
                        tally = piece if tally is None else tally + piece
                        weights.append(piece.astype(jnp.bfloat16))
                    product = jnp.dot(
                        jnp.concatenate(weights, axis=1),
                        both_ref[at : at + step_k, width + head * HEAD : width + (head + 1) * HEAD],
                        preferred_element_type=jnp.float32,
                    )
                    acc = product if acc is None else acc + product
                if base:
                    acc = acc + sums[head] * factors[head]
                    tally = tally + tallies[head] * factors[head]
                sums[head], tallies[head], tops[head] = acc, tally, shifts[head]

        starts, limits = [], []
        for index, away in enumerate(aways):
            qbuf[index] = q_in[index][...]
            start = ((chip ^ away) * 2 + core) * row_count
            limit = [ends_in[index][0]]
            for _ in range(SCALES - 1):
                limit.append(ends_in[index][jnp.minimum(limit[-1] - start, row_count - 1)])
            starts.append(start)
            limits.append(limit)

        def turn(index, carry):
            def pick(values):
                value = values[0]
                for at in range(1, count):
                    value = jnp.where(index == at, values[at], value)
                return value

            limit = [pick([one[at] for one in limits]) for at in range(SCALES)]
            needed = (limit[-1] + step_k - 1) // step_k
            token = pick(starts) + lax.broadcasted_iota(jnp.int32, (row_count, HEAD), 0)
            bound = jnp.full((row_count, HEAD), limit[-1], jnp.int32)
            for value in reversed(limit[:-1]):
                bound = jnp.where(token < value, value, bound)
            room = bound - lax.broadcasted_iota(jnp.int32, (row_count, HEAD), 1)
            for test, base, steps in (
                (needed == 1, 0, 1),
                (needed >= 2, 0, 2),
                (needed == 3, 2 * step_k, 1),
                (needed == 4, 2 * step_k, 2),
            ):

                @pl.when(test)
                def _(base=base, steps=steps):
                    part(index, room, base, steps)

            for head in range(heads):
                obuf[index, :, head * HEAD : (head + 1) * HEAD] = (
                    sums[head] / jnp.sum(tallies[head], axis=1, keepdims=True)
                ).astype(obuf.dtype)
            return carry

        lax.fori_loop(0, count, turn, 0)
        for index in range(count):
            outs[index][...] = obuf[index]

    state = pltpu.VMEM((heads, row_count, HEAD), jnp.float32)
    return pl.pallas_call(
        kernel,
        out_shape=[jax.ShapeDtypeStruct((row_count, width), jnp.bfloat16)] * count,
        in_specs=[SMEM] * count + [VMEM] * (count + 1),
        out_specs=[VMEM] * count,
        scratch_shapes=[
            pltpu.VMEM((count, row_count, width), jnp.bfloat16),
            pltpu.VMEM((count, row_count, width), jnp.bfloat16),
            pltpu.VMEM((heads, row_count, total // 2), jnp.float32),
            state,
            state,
            state,
        ],
        compiler_params=params(30),
        cost_estimate=pl.CostEstimate(
            flops=4 * count * row_count * total * width,
            bytes_accessed=4 * total * width,
            transcendentals=count * row_count * total * heads,
        ),
        name="attend",
    )(*ends, *queries, both)


def weight_gradient(near, far, grad_near, grad_far, chips, width, planes, split):
    row_count = near[0].shape[0]
    full = chips * width
    out_width = grad_near.shape[1]
    group = full // (planes * chips * 2)

    def kernel(*refs):
        pieces = (refs[0:chips], refs[chips : 2 * chips])
        grads = refs[2 * chips : 2 * chips + 2]
        by_plane = refs[2 * chips + 2 : 2 * chips + 2 + planes]
        by_chip = refs[2 * chips + 2 + planes : 3 * chips + 2 + planes]
        turned, left = refs[3 * chips + 2 + planes :]
        chip, core = place()
        here = lax.axis_index("dp")
        for side in range(2):
            for away in range(chips):
                start = pl.multiple_of((chip ^ away) * width, width)
                turned[pl.ds(start, width), side * row_count : (side + 1) * row_count] = (
                    pieces[side][away][...].T
                )

        def product(outs, columns, picks):
            for out, starts in zip(outs, picks):
                for at, start in enumerate(starts):
                    rows = pl.ds(pl.multiple_of((start * 2 + core) * group, group), group)
                    left[at * group : (at + 1) * group, :] = turned[rows, :]
                size = len(starts) * group
                value = jnp.dot(
                    left[:size, :row_count], grads[0][:, columns], preferred_element_type=jnp.float32
                ) + jnp.dot(
                    left[:size, row_count:], grads[1][:, columns], preferred_element_type=jnp.float32
                )
                out[...] = value.astype(out.dtype)

        product(
            by_plane,
            slice(split, out_width),
            [[(here ^ far_) * chips + at for at in range(chips)] for far_ in range(planes)],
        )
        product(
            by_chip,
            slice(0, split),
            [[at * chips + (chip ^ far_) for at in range(planes)] for far_ in range(chips)],
        )

    def shape(rows, columns, away):
        return jax.ShapeDtypeStruct((rows, columns), jnp.float32 if away == 0 else jnp.bfloat16)

    outs = pl.pallas_call(
        kernel,
        out_shape=[shape(chips * group, out_width - split, away) for away in range(planes)]
        + [shape(planes * group, split, away) for away in range(chips)],
        in_specs=[VMEM] * (2 * chips + 2),
        out_specs=[VMEM] * (planes + chips),
        scratch_shapes=[
            pltpu.VMEM((full, 2 * row_count), jnp.bfloat16),
            pltpu.VMEM((max(planes, chips) * group, 2 * row_count), jnp.bfloat16),
        ],
        compiler_params=params(32),
        cost_estimate=pl.CostEstimate(
            flops=2 * full * row_count * out_width,
            bytes_accessed=4 * row_count * out_width,
            transcendentals=0,
        ),
        name="weight_gradient",
    )(*near, *far, grad_near, grad_far)
    return outs[:planes], outs[planes:]


def project(pieces, out_weight, chips, width):
    row_count = pieces[0].shape[0]
    out_width = out_weight.shape[1]

    def kernel(*refs):
        ins, weight, out = refs[:chips], refs[chips], refs[chips + 1]
        chip, _ = place()
        step = min(out_width, 512)
        for column in range(0, out_width, step):
            value = None
            for away in range(chips):
                start = pl.multiple_of((chip ^ away) * width, width)
                part = jnp.dot(
                    ins[away][...],
                    weight[pl.ds(start, width), column : column + step],
                    preferred_element_type=jnp.float32,
                )
                value = part if value is None else value + part
            out[:, column : column + step] = value.astype(out.dtype)

    return pl.pallas_call(
        kernel,
        out_shape=jax.ShapeDtypeStruct((row_count, out_width), jnp.bfloat16),
        in_specs=[VMEM] * (chips + 1),
        out_specs=VMEM,
        compiler_params=params(24),
        cost_estimate=pl.CostEstimate(
            flops=2 * row_count * out_weight.size,
            bytes_accessed=2 * out_weight.size,
            transcendentals=0,
        ),
        name="project",
    )(*pieces, out_weight)


def add_up(own, others, axis, size):
    group = own.shape[0] // size

    def kernel(*refs):
        ins, outs = refs[: 1 + len(others)], refs[1 + len(others) :]
        here = lax.axis_index("dp") if axis == "dp" else place()[0]
        for away in range(size):
            rows = pl.ds(pl.multiple_of((here ^ away) * group, group), group)
            value = ins[0][rows, :]
            for ref in ins[1:]:
                value = value + ref[rows, :].astype(jnp.float32)
            outs[away][...] = value.astype(outs[away].dtype)

    return pl.pallas_call(
        kernel,
        out_shape=[
            jax.ShapeDtypeStruct(
                (group, own.shape[1]), jnp.float32 if away == 0 else jnp.bfloat16
            )
            for away in range(size)
        ],
        in_specs=[VMEM] * (1 + len(others)),
        out_specs=[VMEM] * size,
        compiler_params=params(16),
        name="add_up",
    )(own, *others)


def finish(lefts, rights):
    rows, split = lefts[0].shape
    width = split + rights[0].shape[1]

    def kernel(*refs):
        ins, out = refs[:-1], refs[-1]
        for group, columns in (
            (ins[: len(lefts)], slice(0, split)),
            (ins[len(lefts) :], slice(split, width)),
        ):
            value = group[0][...]
            for ref in group[1:]:
                value = value + ref[...].astype(jnp.float32)
            out[:, columns] = value

    return pl.pallas_call(
        kernel,
        out_shape=jax.ShapeDtypeStruct((rows, width), jnp.float32),
        in_specs=[VMEM] * (len(lefts) + len(rights)),
        out_specs=VMEM,
        compiler_params=params(16),
        name="finish",
    )(*lefts, *rights)


def body(seq, planes, query_rows, key_rows, value_rows, scale_end, out_weight, grad_out):
    chips = seq // 2
    full = query_rows.shape[2]
    width = full // chips

    def over(axis, size, value, mask):
        return lax.ppermute(value, axis, [(i, i ^ mask) for i in range(size)])

    def other_core(value):
        return over("seq", seq, value, 1)

    def spread(pieces):
        return [pieces[0]] + [over("seq", seq, pieces[away], 2 * away) for away in range(1, chips)]

    def meet(pieces):
        return [pieces[0]] + [over("dp", planes, pieces[away], away) for away in range(1, planes)]

    sources = [key_rows[0], value_rows[0]]
    last = cut(sources, [chips - 1], width)
    rest = cut(sources, range(chips - 1), width)
    near = spread([*rest, *last])
    queries = spread(cut([query_rows[0]], range(chips), width))
    ends = spread([scale_end] * chips)
    far = [other_core(piece) for piece in near]
    grad_near = grad_out[0]
    grad_far = other_core(grad_near)
    both = assemble(near, far, chips)
    mine = [None] * chips
    for aways in ([chips - 1], list(range(1, chips - 1)), [0]):
        results = attend([queries[i] for i in aways], [ends[i] for i in aways], aways, both, width)
        for away, piece in zip(aways, results):
            mine[away] = over("seq", seq, piece, 2 * away) if away else piece
    others = [other_core(piece) for piece in mine]
    out_width = out_weight.shape[1]
    split = out_width * 11 // 16
    by_plane, by_chip = weight_gradient(
        mine, others, grad_near, grad_far, chips, width, planes, split
    )
    met = meet(by_plane)
    gathered = spread(by_chip)
    mixed_out = project(mine, out_weight, chips, width)[None]
    lefts = meet(add_up(gathered[0], gathered[1:], "dp", planes))
    rights = spread(add_up(met[0], met[1:], "seq", chips))
    return mixed_out, finish(lefts, rights)


def solution(mesh):
    placed = (
        P("dp", "seq", None),
        P("dp", "seq", None),
        P("dp", "seq", None),
        P("seq"),
        P(),
        P("dp", "seq", None),
    )
    seq, planes = mesh.shape["seq"], mesh.shape["dp"]
    return jax.shard_map(
        functools.partial(body, seq, planes),
        mesh=mesh,
        in_specs=placed,
        out_specs=(P("dp", "seq", None), P(("dp", "seq"), None)),
        check_vma=False,
    )
```

```python
import functools

import jax
import jax.numpy as jnp
from jax import lax
from jax.experimental import pallas as pl
from jax.experimental.pallas import tpu as pltpu
from jax.sharding import PartitionSpec as P


HEAD = 128
FLOOR = -1e30
SCALES = 4
LOG2E = 1.4426950408889634


HBM = pl.BlockSpec(memory_space=pltpu.HBM)
VMEM = pl.BlockSpec(memory_space=pltpu.VMEM)
SMEM = pl.BlockSpec(memory_space=pltpu.SMEM)


def place():
    index = lax.axis_index("seq")
    return index // 2, index % 2


def params(mebibytes):
    return pltpu.CompilerParams(vmem_limit_bytes=mebibytes * 1024 * 1024)


def cut(sources, aways, width):
    row_count = sources[0].shape[0]
    count = len(sources)

    def kernel(*refs):
        ins, outs, sems = refs[:count], refs[count:-1], refs[-1]
        chip, _ = place()
        copies = []
        for out, away in zip(outs, aways):
            columns = pl.ds(pl.multiple_of((chip ^ away) * width, width), width)
            for at, source in enumerate(ins):
                copies.append(
                    pltpu.make_async_copy(
                        source.at[:, columns],
                        out.at[:, at * width : (at + 1) * width],
                        sems.at[len(copies)],
                    )
                )
        for copy in copies:
            copy.start()
        for copy in copies:
            copy.wait()

    shape = jax.ShapeDtypeStruct((row_count, count * width), sources[0].dtype)
    return pl.pallas_call(
        kernel,
        out_shape=[shape] * len(aways),
        in_specs=[HBM] * count,
        out_specs=[VMEM] * len(aways),
        scratch_shapes=[pltpu.SemaphoreType.DMA((count * len(aways),))],
        compiler_params=params(16),
        name="cut",
    )(*(pltpu.with_memory_space_constraint(source, pltpu.HBM) for source in sources))


def assemble(near, far, chips):
    row_count, wide = near[0].shape

    def kernel(*refs):
        pieces, out = (refs[:chips], refs[chips : 2 * chips]), refs[2 * chips]
        chip, core = place()
        for away in range(chips):
            for side in range(2):
                at = (chip ^ away) * 2 + (core ^ side)
                rows = pl.ds(pl.multiple_of(at * row_count, row_count), row_count)
                out[rows, :] = pieces[side][away][...]

    return pl.pallas_call(
        kernel,
        out_shape=jax.ShapeDtypeStruct((2 * chips * row_count, wide), near[0].dtype),
        in_specs=[VMEM] * (2 * chips),
        out_specs=VMEM,
        compiler_params=params(16),
        name="assemble",
    )(*near, *far)


def attend(queries, ends, aways, both, width):
    row_count = queries[0].shape[0]
    total = both.shape[0]
    heads = width // HEAD
    count = len(queries)
    step_k = total // 4
    scale = float(HEAD) ** -0.5 * LOG2E

    def kernel(*refs):
        ends_in = refs[:count]
        q_in = refs[count : 2 * count]
        both_ref = refs[2 * count]
        outs = refs[2 * count + 1 : 3 * count + 1]
        qbuf, obuf, sbuf, sums, tallies, tops = refs[3 * count + 1 :]
        chip, core = place()

        def part(index, room, base, steps):
            shifts, factors = [], []
            for head in range(heads):
                columns = slice(head * HEAD, (head + 1) * HEAD)
                query = qbuf[index, :, columns]
                top = None
                for at in range(base, base + steps * step_k, step_k):
                    score = lax.dot_general(
                        query,
                        both_ref[at : at + step_k, columns],
                        (((1,), (1,)), ((), ())),
                        preferred_element_type=jnp.float32,
                    )
                    for key in range(0, step_k, HEAD):
                        piece = jnp.where(room > at + key, score[:, key : key + HEAD], FLOOR)
                        sbuf[head, :, at - base + key : at - base + key + HEAD] = piece
                        top = piece if top is None else jnp.maximum(top, piece)
                shift = jnp.broadcast_to(jnp.max(top, axis=1, keepdims=True), top.shape) * scale
                if base:
                    before = tops[head]
                    shift = jnp.maximum(before, shift)
                    factors.append(jnp.exp2(before - shift))
                shifts.append(shift)
            for head in range(heads):
                tally = acc = None
                for at in range(base, base + steps * step_k, step_k):
                    weights = []
                    for key in range(0, step_k, HEAD):
                        piece = sbuf[head, :, at - base + key : at - base + key + HEAD]
                        piece = jnp.exp2(piece * scale - shifts[head])
                        tally = piece if tally is None else tally + piece
                        weights.append(piece.astype(jnp.bfloat16))
                    product = jnp.dot(
                        jnp.concatenate(weights, axis=1),
                        both_ref[at : at + step_k, width + head * HEAD : width + (head + 1) * HEAD],
                        preferred_element_type=jnp.float32,
                    )
                    acc = product if acc is None else acc + product
                if base:
                    acc = acc + sums[head] * factors[head]
                    tally = tally + tallies[head] * factors[head]
                sums[head], tallies[head], tops[head] = acc, tally, shifts[head]

        starts, limits = [], []
        for index, away in enumerate(aways):
            qbuf[index] = q_in[index][...]
            start = ((chip ^ away) * 2 + core) * row_count
            limit = [ends_in[index][0]]
            for _ in range(SCALES - 1):
                limit.append(ends_in[index][jnp.minimum(limit[-1] - start, row_count - 1)])
            starts.append(start)
            limits.append(limit)

        def turn(index, carry):
            def pick(values):
                value = values[0]
                for at in range(1, count):
                    value = jnp.where(index == at, values[at], value)
                return value

            limit = [pick([one[at] for one in limits]) for at in range(SCALES)]
            needed = (limit[-1] + step_k - 1) // step_k
            token = pick(starts) + lax.broadcasted_iota(jnp.int32, (row_count, HEAD), 0)
            bound = jnp.full((row_count, HEAD), limit[-1], jnp.int32)
            for value in reversed(limit[:-1]):
                bound = jnp.where(token < value, value, bound)
            room = bound - lax.broadcasted_iota(jnp.int32, (row_count, HEAD), 1)
            for test, base, steps in (
                (needed == 1, 0, 1),
                (needed >= 2, 0, 2),
                (needed == 3, 2 * step_k, 1),
                (needed == 4, 2 * step_k, 2),
            ):

                @pl.when(test)
                def _(base=base, steps=steps):
                    part(index, room, base, steps)

            for head in range(heads):
                obuf[index, :, head * HEAD : (head + 1) * HEAD] = (
                    sums[head] / jnp.sum(tallies[head], axis=1, keepdims=True)
                ).astype(obuf.dtype)
            return carry

        lax.fori_loop(0, count, turn, 0)
        for index in range(count):
            outs[index][...] = obuf[index]

    state = pltpu.VMEM((heads, row_count, HEAD), jnp.float32)
    return pl.pallas_call(
        kernel,
        out_shape=[jax.ShapeDtypeStruct((row_count, width), jnp.bfloat16)] * count,
        in_specs=[SMEM] * count + [VMEM] * (count + 1),
        out_specs=[VMEM] * count,
        scratch_shapes=[
            pltpu.VMEM((count, row_count, width), jnp.bfloat16),
            pltpu.VMEM((count, row_count, width), jnp.bfloat16),
            pltpu.VMEM((heads, row_count, total // 2), jnp.float32),
            state,
            state,
            state,
        ],
        compiler_params=params(30),
        cost_estimate=pl.CostEstimate(
            flops=4 * count * row_count * total * width,
            bytes_accessed=4 * total * width,
            transcendentals=count * row_count * total * heads,
        ),
        name="attend",
    )(*ends, *queries, both)


def turn_over(near, far, chips, width):
    row_count = near[0].shape[0]

    def kernel(*refs):
        pieces, out = (refs[:chips], refs[chips : 2 * chips]), refs[2 * chips]
        chip, _ = place()
        for side in range(2):
            for away in range(chips):
                start = pl.multiple_of((chip ^ away) * width, width)
                out[pl.ds(start, width), side * row_count : (side + 1) * row_count] = (
                    pieces[side][away][...].T
                )

    return kernel, jax.ShapeDtypeStruct((chips * width, 2 * row_count), near[0].dtype)


def weight_gradient(turned, grad_near, grad_far, columns, axis, chips, planes, pieces=None):
    row_count = grad_near.shape[0]
    if pieces is None:
        turn, shape, sources = None, turned.shape, [turned]
    else:
        turn, target = turn_over(*pieces)
        shape, sources = target.shape, [*pieces[0], *pieces[1]]
    group = shape[0] // (planes * chips * 2)
    size = planes if axis == "dp" else chips
    other = chips if axis == "dp" else planes

    def kernel(*refs):
        ins, rest = refs[: len(sources)], refs[len(sources) :]
        grads, outs, left = rest[:2], rest[2 : 2 + size], rest[-1]
        flat = ins[0]
        if turn is not None:
            flat = rest[2 + size]
            turn(*ins, flat)
        chip, core = place()
        plane = lax.axis_index("dp")
        for away, out in enumerate(outs):
            for at in range(other):
                start = (plane ^ away) * chips + at if axis == "dp" else at * chips + (chip ^ away)
                rows = pl.ds(pl.multiple_of((start * 2 + core) * group, group), group)
                left[at * group : (at + 1) * group, :] = flat[rows, :]
            value = jnp.dot(
                left[:, :row_count], grads[0][:, columns], preferred_element_type=jnp.float32
            ) + jnp.dot(
                left[:, row_count:], grads[1][:, columns], preferred_element_type=jnp.float32
            )
            out[...] = value.astype(out.dtype)

    width = columns.stop - columns.start
    shapes = [
        jax.ShapeDtypeStruct((other * group, width), jnp.float32 if away == 0 else jnp.bfloat16)
        for away in range(size)
    ]
    if turn is not None:
        shapes.append(target)
    return pl.pallas_call(
        kernel,
        out_shape=shapes,
        in_specs=[VMEM] * (len(sources) + 2),
        out_specs=[VMEM] * len(shapes),
        scratch_shapes=[pltpu.VMEM((other * group, 2 * row_count), jnp.bfloat16)],
        compiler_params=params(32),
        cost_estimate=pl.CostEstimate(
            flops=2 * shape[0] * row_count * width,
            bytes_accessed=4 * row_count * width,
            transcendentals=0,
        ),
        name="weight_gradient",
    )(*sources, grad_near, grad_far)


def project(pieces, out_weight, chips, width):
    row_count = pieces[0].shape[0]
    out_width = out_weight.shape[1]

    def kernel(*refs):
        ins, weight, out = refs[:chips], refs[chips], refs[chips + 1]
        chip, _ = place()
        step = min(out_width, 512)
        for column in range(0, out_width, step):
            value = None
            for away in range(chips):
                start = pl.multiple_of((chip ^ away) * width, width)
                part = jnp.dot(
                    ins[away][...],
                    weight[pl.ds(start, width), column : column + step],
                    preferred_element_type=jnp.float32,
                )
                value = part if value is None else value + part
            out[:, column : column + step] = value.astype(out.dtype)

    return pl.pallas_call(
        kernel,
        out_shape=jax.ShapeDtypeStruct((row_count, out_width), jnp.bfloat16),
        in_specs=[VMEM] * (chips + 1),
        out_specs=VMEM,
        compiler_params=params(24),
        cost_estimate=pl.CostEstimate(
            flops=2 * row_count * out_weight.size,
            bytes_accessed=2 * out_weight.size,
            transcendentals=0,
        ),
        name="project",
    )(*pieces, out_weight)


def add_up(own, others, axis, size):
    group = own.shape[0] // size

    def kernel(*refs):
        ins, outs = refs[: 1 + len(others)], refs[1 + len(others) :]
        here = lax.axis_index("dp") if axis == "dp" else place()[0]
        for away in range(size):
            rows = pl.ds(pl.multiple_of((here ^ away) * group, group), group)
            value = ins[0][rows, :]
            for ref in ins[1:]:
                value = value + ref[rows, :].astype(jnp.float32)
            outs[away][...] = value.astype(outs[away].dtype)

    return pl.pallas_call(
        kernel,
        out_shape=[
            jax.ShapeDtypeStruct(
                (group, own.shape[1]), jnp.float32 if away == 0 else jnp.bfloat16
            )
            for away in range(size)
        ],
        in_specs=[VMEM] * (1 + len(others)),
        out_specs=[VMEM] * size,
        compiler_params=params(16),
        name="add_up",
    )(own, *others)


def finish(lefts, rights):
    rows, split = lefts[0].shape
    width = split + rights[0].shape[1]

    def kernel(*refs):
        ins, out = refs[:-1], refs[-1]
        for group, columns in (
            (ins[: len(lefts)], slice(0, split)),
            (ins[len(lefts) :], slice(split, width)),
        ):
            value = group[0][...]
            for ref in group[1:]:
                value = value + ref[...].astype(jnp.float32)
            out[:, columns] = value

    return pl.pallas_call(
        kernel,
        out_shape=jax.ShapeDtypeStruct((rows, width), jnp.float32),
        in_specs=[VMEM] * (len(lefts) + len(rights)),
        out_specs=VMEM,
        compiler_params=params(16),
        name="finish",
    )(*lefts, *rights)


def body(seq, planes, query_rows, key_rows, value_rows, scale_end, out_weight, grad_out):
    chips = seq // 2
    full = query_rows.shape[2]
    width = full // chips

    def over(axis, size, value, mask):
        return lax.ppermute(value, axis, [(i, i ^ mask) for i in range(size)])

    def other_core(value):
        return over("seq", seq, value, 1)

    def spread(pieces):
        return [pieces[0]] + [over("seq", seq, pieces[away], 2 * away) for away in range(1, chips)]

    def meet(pieces):
        return [pieces[0]] + [over("dp", planes, pieces[away], away) for away in range(1, planes)]

    sources = [key_rows[0], value_rows[0]]
    last = cut(sources, [chips - 1], width)
    rest = cut(sources, range(chips - 1), width)
    near = spread([*rest, *last])
    queries = spread(cut([query_rows[0]], range(chips), width))
    ends = spread([scale_end] * chips)
    far = [other_core(piece) for piece in near]
    grad_near = grad_out[0]
    grad_far = other_core(grad_near)
    both = assemble(near, far, chips)
    mine = [None] * chips
    for aways in ([chips - 1], list(range(1, chips - 1)), [0]):
        results = attend([queries[i] for i in aways], [ends[i] for i in aways], aways, both, width)
        for away, piece in zip(aways, results):
            mine[away] = over("seq", seq, piece, 2 * away) if away else piece
    others = [other_core(piece) for piece in mine]
    out_width = out_weight.shape[1]
    split = out_width * 11 // 16
    grads = (grad_near, grad_far)
    *by_chip, turned = weight_gradient(
        None, *grads, slice(0, split), "seq", chips, planes, (mine, others, chips, width)
    )
    gathered = spread(by_chip)
    by_plane = weight_gradient(
        turned, *grads, slice(split, out_width), "dp", chips, planes
    )
    met = meet(by_plane)
    mixed_out = project(mine, out_weight, chips, width)[None]
    lefts = meet(add_up(gathered[0], gathered[1:], "dp", planes))
    rights = spread(add_up(met[0], met[1:], "seq", chips))
    return mixed_out, finish(lefts, rights)


def solution(mesh):
    placed = (
        P("dp", "seq", None),
        P("dp", "seq", None),
        P("dp", "seq", None),
        P("seq"),
        P(),
        P("dp", "seq", None),
    )
    seq, planes = mesh.shape["seq"], mesh.shape["dp"]
    return jax.shard_map(
        functools.partial(body, seq, planes),
        mesh=mesh,
        in_specs=placed,
        out_specs=(P("dp", "seq", None), P(("dp", "seq"), None)),
        check_vma=False,
    )
```

```python
import functools

import jax
import jax.numpy as jnp
from jax import lax
from jax.experimental import pallas as pl
from jax.experimental.pallas import tpu as pltpu
from jax.sharding import PartitionSpec as P


HEAD = 128
FLOOR = -1e30
SCALES = 4
LOG2E = 1.4426950408889634


HBM = pl.BlockSpec(memory_space=pltpu.HBM)
VMEM = pl.BlockSpec(memory_space=pltpu.VMEM)
SMEM = pl.BlockSpec(memory_space=pltpu.SMEM)


def place():
    index = lax.axis_index("seq")
    return index // 2, index % 2


def params(mebibytes):
    return pltpu.CompilerParams(vmem_limit_bytes=mebibytes * 1024 * 1024)


def cut(sources, aways, width):
    row_count = sources[0].shape[0]
    count = len(sources)

    def kernel(*refs):
        ins, outs, sems = refs[:count], refs[count:-1], refs[-1]
        chip, _ = place()
        copies = []
        for out, away in zip(outs, aways):
            columns = pl.ds(pl.multiple_of((chip ^ away) * width, width), width)
            for at, source in enumerate(ins):
                copies.append(
                    pltpu.make_async_copy(
                        source.at[:, columns],
                        out.at[:, at * width : (at + 1) * width],
                        sems.at[len(copies)],
                    )
                )
        for copy in copies:
            copy.start()
        for copy in copies:
            copy.wait()

    shape = jax.ShapeDtypeStruct((row_count, count * width), sources[0].dtype)
    return pl.pallas_call(
        kernel,
        out_shape=[shape] * len(aways),
        in_specs=[HBM] * count,
        out_specs=[VMEM] * len(aways),
        scratch_shapes=[pltpu.SemaphoreType.DMA((count * len(aways),))],
        compiler_params=params(16),
        name="cut",
    )(*(pltpu.with_memory_space_constraint(source, pltpu.HBM) for source in sources))


def assemble(near, far, chips):
    row_count, wide = near[0].shape

    def kernel(*refs):
        pieces, out = (refs[:chips], refs[chips : 2 * chips]), refs[2 * chips]
        chip, core = place()
        for away in range(chips):
            for side in range(2):
                at = (chip ^ away) * 2 + (core ^ side)
                rows = pl.ds(pl.multiple_of(at * row_count, row_count), row_count)
                out[rows, :] = pieces[side][away][...]

    return pl.pallas_call(
        kernel,
        out_shape=jax.ShapeDtypeStruct((2 * chips * row_count, wide), near[0].dtype),
        in_specs=[VMEM] * (2 * chips),
        out_specs=VMEM,
        compiler_params=params(16),
        name="assemble",
    )(*near, *far)


def attend(queries, ends, aways, both, width):
    row_count = queries[0].shape[0]
    total = both.shape[0]
    heads = width // HEAD
    count = len(queries)
    step_k = total // 4
    scale = float(HEAD) ** -0.5 * LOG2E

    def kernel(*refs):
        ends_in = refs[:count]
        q_in = refs[count : 2 * count]
        both_ref = refs[2 * count]
        outs = refs[2 * count + 1 : 3 * count + 1]
        qbuf, obuf, sbuf, sums, tallies, tops = refs[3 * count + 1 :]
        chip, core = place()

        def part(index, room, base, steps):
            shifts, factors = [], []
            for head in range(heads):
                columns = slice(head * HEAD, (head + 1) * HEAD)
                query = q_in[0][:, columns] if count == 1 else qbuf[index, :, columns]
                top = None
                for at in range(base, base + steps * step_k, step_k):
                    score = lax.dot_general(
                        query,
                        both_ref[at : at + step_k, columns],
                        (((1,), (1,)), ((), ())),
                        preferred_element_type=jnp.float32,
                    )
                    for key in range(0, step_k, HEAD):
                        piece = jnp.where(room > at + key, score[:, key : key + HEAD], FLOOR)
                        sbuf[head, :, at - base + key : at - base + key + HEAD] = piece
                        top = piece if top is None else jnp.maximum(top, piece)
                shift = jnp.broadcast_to(jnp.max(top, axis=1, keepdims=True), top.shape) * scale
                if base:
                    before = tops[head]
                    shift = jnp.maximum(before, shift)
                    factors.append(jnp.exp2(before - shift))
                shifts.append(shift)
            for head in range(heads):
                tally = acc = None
                for at in range(base, base + steps * step_k, step_k):
                    weights = []
                    for key in range(0, step_k, HEAD):
                        piece = sbuf[head, :, at - base + key : at - base + key + HEAD]
                        piece = jnp.exp2(piece * scale - shifts[head])
                        tally = piece if tally is None else tally + piece
                        weights.append(piece.astype(jnp.bfloat16))
                    product = jnp.dot(
                        jnp.concatenate(weights, axis=1),
                        both_ref[at : at + step_k, width + head * HEAD : width + (head + 1) * HEAD],
                        preferred_element_type=jnp.float32,
                    )
                    acc = product if acc is None else acc + product
                if base:
                    acc = acc + sums[head] * factors[head]
                    tally = tally + tallies[head] * factors[head]
                sums[head], tallies[head], tops[head] = acc, tally, shifts[head]

        starts, limits = [], []
        for index, away in enumerate(aways):
            if count > 1:
                qbuf[index] = q_in[index][...]
            start = ((chip ^ away) * 2 + core) * row_count
            limit = [ends_in[index][0]]
            for _ in range(SCALES - 1):
                limit.append(ends_in[index][jnp.minimum(limit[-1] - start, row_count - 1)])
            starts.append(start)
            limits.append(limit)

        def turn(index, carry):
            def pick(values):
                value = values[0]
                for at in range(1, count):
                    value = jnp.where(index == at, values[at], value)
                return value

            limit = [pick([one[at] for one in limits]) for at in range(SCALES)]
            needed = (limit[-1] + step_k - 1) // step_k
            token = pick(starts) + lax.broadcasted_iota(jnp.int32, (row_count, HEAD), 0)
            bound = jnp.full((row_count, HEAD), limit[-1], jnp.int32)
            for value in reversed(limit[:-1]):
                bound = jnp.where(token < value, value, bound)
            room = bound - lax.broadcasted_iota(jnp.int32, (row_count, HEAD), 1)
            for test, base, steps in (
                (needed == 1, 0, 1),
                (needed >= 2, 0, 2),
                (needed == 3, 2 * step_k, 1),
                (needed == 4, 2 * step_k, 2),
            ):

                @pl.when(test)
                def _(base=base, steps=steps):
                    part(index, room, base, steps)

            for head in range(heads):
                value = sums[head] / jnp.sum(tallies[head], axis=1, keepdims=True)
                columns = slice(head * HEAD, (head + 1) * HEAD)
                if count == 1:
                    outs[0][:, columns] = value.astype(obuf.dtype)
                else:
                    obuf[index, :, columns] = value.astype(obuf.dtype)
            return carry

        if count == 1:
            turn(0, 0)
            return
        lax.fori_loop(0, count, turn, 0)
        for index in range(count):
            outs[index][...] = obuf[index]

    state = pltpu.VMEM((heads, row_count, HEAD), jnp.float32)
    return pl.pallas_call(
        kernel,
        out_shape=[jax.ShapeDtypeStruct((row_count, width), jnp.bfloat16)] * count,
        in_specs=[SMEM] * count + [VMEM] * (count + 1),
        out_specs=[VMEM] * count,
        scratch_shapes=[
            pltpu.VMEM((count, row_count, width), jnp.bfloat16),
            pltpu.VMEM((count, row_count, width), jnp.bfloat16),
            pltpu.VMEM((heads, row_count, total // 2), jnp.float32),
            state,
            state,
            state,
        ],
        compiler_params=params(30),
        cost_estimate=pl.CostEstimate(
            flops=4 * count * row_count * total * width,
            bytes_accessed=4 * total * width,
            transcendentals=count * row_count * total * heads,
        ),
        name="attend",
    )(*ends, *queries, both)


def turn_over(near, far, chips, width):
    row_count = near[0].shape[0]

    def kernel(*refs):
        pieces, out = (refs[:chips], refs[chips : 2 * chips]), refs[2 * chips]
        chip, _ = place()
        for side in range(2):
            for away in range(chips):
                start = pl.multiple_of((chip ^ away) * width, width)
                out[pl.ds(start, width), side * row_count : (side + 1) * row_count] = (
                    pieces[side][away][...].T
                )

    return kernel, jax.ShapeDtypeStruct((chips * width, 2 * row_count), near[0].dtype)


def weight_gradient(turned, grad_near, grad_far, columns, axis, chips, planes, pieces=None):
    row_count = grad_near.shape[0]
    if pieces is None:
        turn, shape, sources = None, turned.shape, [turned]
    else:
        turn, target = turn_over(*pieces)
        shape, sources = target.shape, [*pieces[0], *pieces[1]]
    group = shape[0] // (planes * chips * 2)
    size = planes if axis == "dp" else chips
    other = chips if axis == "dp" else planes

    def kernel(*refs):
        ins, rest = refs[: len(sources)], refs[len(sources) :]
        grads, outs, left = rest[:2], rest[2 : 2 + size], rest[-1]
        flat = ins[0]
        if turn is not None:
            flat = rest[2 + size]
            turn(*ins, flat)
        chip, core = place()
        plane = lax.axis_index("dp")
        for away in range(size):
            for at in range(other):
                start = (plane ^ away) * chips + at if axis == "dp" else at * chips + (chip ^ away)
                rows = pl.ds(pl.multiple_of((start * 2 + core) * group, group), group)
                target = (away * other + at) * group
                left[target : target + group, :] = flat[rows, :]
        for first in range(columns.start, columns.stop, 512):
            part = slice(first, min(first + 512, columns.stop))
            value = jnp.dot(
                left[:, :row_count], grads[0][:, part], preferred_element_type=jnp.float32
            ) + jnp.dot(left[:, row_count:], grads[1][:, part], preferred_element_type=jnp.float32)
            for away, out in enumerate(outs):
                rows = slice(away * other * group, (away + 1) * other * group)
                out[:, part.start - columns.start : part.stop - columns.start] = value[rows].astype(
                    out.dtype
                )

    width = columns.stop - columns.start
    shapes = [
        jax.ShapeDtypeStruct((other * group, width), jnp.float32 if away == 0 else jnp.bfloat16)
        for away in range(size)
    ]
    if turn is not None:
        shapes.append(target)
    return pl.pallas_call(
        kernel,
        out_shape=shapes,
        in_specs=[VMEM] * (len(sources) + 2),
        out_specs=[VMEM] * len(shapes),
        scratch_shapes=[pltpu.VMEM((size * other * group, 2 * row_count), jnp.bfloat16)],
        compiler_params=params(32),
        cost_estimate=pl.CostEstimate(
            flops=2 * shape[0] * row_count * width,
            bytes_accessed=4 * row_count * width,
            transcendentals=0,
        ),
        name="weight_gradient",
    )(*sources, grad_near, grad_far)


def project(pieces, out_weight, chips, width):
    row_count = pieces[0].shape[0]
    out_width = out_weight.shape[1]

    def kernel(*refs):
        ins, weight, out = refs[:chips], refs[chips], refs[chips + 1]
        chip, _ = place()
        step = min(out_width, 512)
        for column in range(0, out_width, step):
            value = None
            for away in range(chips):
                start = pl.multiple_of((chip ^ away) * width, width)
                part = jnp.dot(
                    ins[away][...],
                    weight[pl.ds(start, width), column : column + step],
                    preferred_element_type=jnp.float32,
                )
                value = part if value is None else value + part
            out[:, column : column + step] = value.astype(out.dtype)

    return pl.pallas_call(
        kernel,
        out_shape=jax.ShapeDtypeStruct((row_count, out_width), jnp.bfloat16),
        in_specs=[VMEM] * (chips + 1),
        out_specs=VMEM,
        compiler_params=params(24),
        cost_estimate=pl.CostEstimate(
            flops=2 * row_count * out_weight.size,
            bytes_accessed=2 * out_weight.size,
            transcendentals=0,
        ),
        name="project",
    )(*pieces, out_weight)


def add_up(own, others, axis, size):
    group = own.shape[0] // size

    def kernel(*refs):
        ins, outs = refs[: 1 + len(others)], refs[1 + len(others) :]
        here = lax.axis_index("dp") if axis == "dp" else place()[0]
        for away in range(size):
            rows = pl.ds(pl.multiple_of((here ^ away) * group, group), group)
            value = ins[0][rows, :]
            for ref in ins[1:]:
                value = value + ref[rows, :].astype(jnp.float32)
            outs[away][...] = value.astype(outs[away].dtype)

    return pl.pallas_call(
        kernel,
        out_shape=[
            jax.ShapeDtypeStruct(
                (group, own.shape[1]), jnp.float32 if away == 0 else jnp.bfloat16
            )
            for away in range(size)
        ],
        in_specs=[VMEM] * (1 + len(others)),
        out_specs=[VMEM] * size,
        compiler_params=params(16),
        name="add_up",
    )(own, *others)


def finish(lefts, rights):
    rows, split = lefts[0].shape
    width = split + rights[0].shape[1]

    def kernel(*refs):
        ins, out = refs[:-1], refs[-1]
        for group, columns in (
            (ins[: len(lefts)], slice(0, split)),
            (ins[len(lefts) :], slice(split, width)),
        ):
            value = group[0][...]
            for ref in group[1:]:
                value = value + ref[...].astype(jnp.float32)
            out[:, columns] = value

    return pl.pallas_call(
        kernel,
        out_shape=jax.ShapeDtypeStruct((rows, width), jnp.float32),
        in_specs=[VMEM] * (len(lefts) + len(rights)),
        out_specs=VMEM,
        compiler_params=params(16),
        name="finish",
    )(*lefts, *rights)


def body(seq, planes, query_rows, key_rows, value_rows, scale_end, out_weight, grad_out):
    chips = seq // 2
    full = query_rows.shape[2]
    width = full // chips

    def over(axis, size, value, mask):
        return lax.ppermute(value, axis, [(i, i ^ mask) for i in range(size)])

    def other_core(value):
        return over("seq", seq, value, 1)

    def spread(pieces):
        return [pieces[0]] + [over("seq", seq, pieces[away], 2 * away) for away in range(1, chips)]

    def meet(pieces):
        return [pieces[0]] + [over("dp", planes, pieces[away], away) for away in range(1, planes)]

    sources = [key_rows[0], value_rows[0]]
    last = cut(sources, [chips - 1], width)
    rest = cut(sources, range(chips - 1), width)
    near = spread([*rest, *last])
    queries = spread(cut([query_rows[0]], range(chips), width))
    ends = spread([scale_end] * chips)
    far = [other_core(piece) for piece in near]
    grad_near = grad_out[0]
    grad_far = other_core(grad_near)
    both = assemble(near, far, chips)
    mine = [None] * chips
    for aways in ([chips - 1], list(range(1, chips - 1)), [0]):
        results = attend([queries[i] for i in aways], [ends[i] for i in aways], aways, both, width)
        for away, piece in zip(aways, results):
            mine[away] = over("seq", seq, piece, 2 * away) if away else piece
    others = [other_core(piece) for piece in mine]
    out_width = out_weight.shape[1]
    split = out_width * 11 // 16
    grads = (grad_near, grad_far)
    *by_chip, turned = weight_gradient(
        None, *grads, slice(0, split), "seq", chips, planes, (mine, others, chips, width)
    )
    gathered = spread(by_chip)
    by_plane = weight_gradient(
        turned, *grads, slice(split, out_width), "dp", chips, planes
    )
    met = meet(by_plane)
    mixed_out = project(mine, out_weight, chips, width)[None]
    lefts = meet(add_up(gathered[0], gathered[1:], "dp", planes))
    rights = spread(add_up(met[0], met[1:], "seq", chips))
    return mixed_out, finish(lefts, rights)


def solution(mesh):
    placed = (
        P("dp", "seq", None),
        P("dp", "seq", None),
        P("dp", "seq", None),
        P("seq"),
        P(),
        P("dp", "seq", None),
    )
    seq, planes = mesh.shape["seq"], mesh.shape["dp"]
    return jax.shard_map(
        functools.partial(body, seq, planes),
        mesh=mesh,
        in_specs=placed,
        out_specs=(P("dp", "seq", None), P(("dp", "seq"), None)),
        check_vma=False,
    )
```

```python
import functools

import jax
import jax.numpy as jnp
from jax import lax
from jax.experimental import pallas as pl
from jax.experimental.pallas import tpu as pltpu
from jax.sharding import PartitionSpec as P


HEAD = 128
FLOOR = -1e30
LOG2E = 1.4426950408889634


HBM = pl.BlockSpec(memory_space=pltpu.HBM)
VMEM = pl.BlockSpec(memory_space=pltpu.VMEM)


def place():
    index = lax.axis_index("seq")
    return index // 2, index % 2


def params(mebibytes):
    return pltpu.CompilerParams(vmem_limit_bytes=mebibytes * 1024 * 1024)


def cut(sources, aways, width):
    row_count = sources[0].shape[0]
    count = len(sources)

    def kernel(*refs):
        ins, outs, sems = refs[:count], refs[count:-1], refs[-1]
        chip, _ = place()
        copies = []
        for out, away in zip(outs, aways):
            columns = pl.ds(pl.multiple_of((chip ^ away) * width, width), width)
            for at, source in enumerate(ins):
                copies.append(
                    pltpu.make_async_copy(
                        source.at[:, columns],
                        out.at[:, at * width : (at + 1) * width],
                        sems.at[len(copies)],
                    )
                )
        for copy in copies:
            copy.start()
        for copy in copies:
            copy.wait()

    shape = jax.ShapeDtypeStruct((row_count, count * width), sources[0].dtype)
    return pl.pallas_call(
        kernel,
        out_shape=[shape] * len(aways),
        in_specs=[HBM] * count,
        out_specs=[VMEM] * len(aways),
        scratch_shapes=[pltpu.SemaphoreType.DMA((count * len(aways),))],
        compiler_params=params(16),
        name="cut",
    )(*(pltpu.with_memory_space_constraint(source, pltpu.HBM) for source in sources))


def assemble(near, far, chips):
    row_count, wide = near[0].shape

    def kernel(*refs):
        pieces, out = (refs[:chips], refs[chips : 2 * chips]), refs[2 * chips]
        chip, core = place()
        for away in range(chips):
            for side in range(2):
                at = (chip ^ away) * 2 + (core ^ side)
                rows = pl.ds(pl.multiple_of(at * row_count, row_count), row_count)
                out[rows, :] = pieces[side][away][...]

    return pl.pallas_call(
        kernel,
        out_shape=jax.ShapeDtypeStruct((2 * chips * row_count, wide), near[0].dtype),
        in_specs=[VMEM] * (2 * chips),
        out_specs=VMEM,
        compiler_params=params(16),
        name="assemble",
    )(*near, *far)


def attend(queries, ends, both, width):
    row_count = queries[0].shape[0]
    total = both.shape[0]
    heads = width // HEAD
    count = len(queries)
    step_k = total // 4
    scale = float(HEAD) ** -0.5 * LOG2E

    def kernel(*refs):
        ends_in = refs[:count]
        q_in = refs[count : 2 * count]
        both_ref = refs[2 * count]
        outs = refs[2 * count + 1 : 3 * count + 1]
        qbuf, obuf, sbuf, sums, tallies, tops = refs[3 * count + 1 :]

        def part(index, room, base, steps):
            shifts, factors = [], []
            for head in range(heads):
                columns = slice(head * HEAD, (head + 1) * HEAD)
                query = q_in[0][:, columns] if count == 1 else qbuf[index, :, columns]
                top = None
                for at in range(base, base + steps * step_k, step_k):
                    score = lax.dot_general(
                        query,
                        both_ref[at : at + step_k, columns],
                        (((1,), (1,)), ((), ())),
                        preferred_element_type=jnp.float32,
                    )
                    for key in range(0, step_k, HEAD):
                        piece = jnp.where(room > at + key, score[:, key : key + HEAD], FLOOR)
                        sbuf[head, :, at - base + key : at - base + key + HEAD] = piece
                        top = piece if top is None else jnp.maximum(top, piece)
                shift = jnp.broadcast_to(jnp.max(top, axis=1, keepdims=True), top.shape) * scale
                if base:
                    before = tops[head]
                    shift = jnp.maximum(before, shift)
                    factors.append(jnp.exp2(before - shift))
                shifts.append(shift)
            for head in range(heads):
                tally = acc = None
                for at in range(base, base + steps * step_k, step_k):
                    weights = []
                    for key in range(0, step_k, HEAD):
                        piece = sbuf[head, :, at - base + key : at - base + key + HEAD]
                        piece = jnp.exp2(piece * scale - shifts[head])
                        tally = piece if tally is None else tally + piece
                        weights.append(piece.astype(jnp.bfloat16))
                    product = jnp.dot(
                        jnp.concatenate(weights, axis=1),
                        both_ref[at : at + step_k, width + head * HEAD : width + (head + 1) * HEAD],
                        preferred_element_type=jnp.float32,
                    )
                    acc = product if acc is None else acc + product
                if base:
                    acc = acc + sums[head] * factors[head]
                    tally = tally + tallies[head] * factors[head]
                sums[head], tallies[head], tops[head] = acc, tally, shifts[head]

        for index in range(count):
            if count > 1:
                qbuf[index] = q_in[index][...]

        def turn(index, carry):
            end = ends_in[0][...]
            for at in range(1, count):
                end = jnp.where(index == at, ends_in[at][...], end)
            end = end.astype(jnp.float32)
            reach = jnp.max(end)
            bound = jnp.concatenate(
                [
                    jnp.broadcast_to(end[at : at + 1], (HEAD, HEAD)).T
                    for at in range(row_count // HEAD)
                ],
                axis=0,
            )
            lane = lax.broadcasted_iota(jnp.int32, (row_count, HEAD), 1)
            room = bound - lane.astype(jnp.float32)
            for test, base, steps in (
                (reach <= step_k, 0, 1),
                (reach > step_k, 0, 2),
                ((reach > 2 * step_k) & (reach <= 3 * step_k), 2 * step_k, 1),
                (reach > 3 * step_k, 2 * step_k, 2),
            ):

                @pl.when(test)
                def _(base=base, steps=steps):
                    part(index, room, base, steps)

            for head in range(heads):
                value = sums[head] / jnp.sum(tallies[head], axis=1, keepdims=True)
                columns = slice(head * HEAD, (head + 1) * HEAD)
                if count == 1:
                    outs[0][:, columns] = value.astype(obuf.dtype)
                else:
                    obuf[index, :, columns] = value.astype(obuf.dtype)
            return carry

        if count == 1:
            turn(0, 0)
            return
        lax.fori_loop(0, count, turn, 0)
        for index in range(count):
            outs[index][...] = obuf[index]

    state = pltpu.VMEM((heads, row_count, HEAD), jnp.float32)
    return pl.pallas_call(
        kernel,
        out_shape=[jax.ShapeDtypeStruct((row_count, width), jnp.bfloat16)] * count,
        in_specs=[VMEM] * (2 * count + 1),
        out_specs=[VMEM] * count,
        scratch_shapes=[
            pltpu.VMEM((count, row_count, width), jnp.bfloat16),
            pltpu.VMEM((count, row_count, width), jnp.bfloat16),
            pltpu.VMEM((heads, row_count, total // 2), jnp.float32),
            state,
            state,
            state,
        ],
        compiler_params=params(30),
        cost_estimate=pl.CostEstimate(
            flops=4 * count * row_count * total * width,
            bytes_accessed=4 * total * width,
            transcendentals=count * row_count * total * heads,
        ),
        name="attend",
    )(*ends, *queries, both)


def turn_over(near, far, chips, width):
    row_count = near[0].shape[0]

    def kernel(*refs):
        pieces, out = (refs[:chips], refs[chips : 2 * chips]), refs[2 * chips]
        chip, _ = place()
        for side in range(2):
            for away in range(chips):
                start = pl.multiple_of((chip ^ away) * width, width)
                out[pl.ds(start, width), side * row_count : (side + 1) * row_count] = (
                    pieces[side][away][...].T
                )

    return kernel, jax.ShapeDtypeStruct((chips * width, 2 * row_count), near[0].dtype)


def weight_gradient(turned, grad_near, grad_far, columns, axis, chips, planes, pieces=None):
    row_count = grad_near.shape[0]
    if pieces is None:
        turn, shape, sources = None, turned.shape, [turned]
    else:
        turn, target = turn_over(*pieces)
        shape, sources = target.shape, [*pieces[0], *pieces[1]]
    group = shape[0] // (planes * chips * 2)
    size = planes if axis == "dp" else chips
    other = chips if axis == "dp" else planes

    def kernel(*refs):
        ins, rest = refs[: len(sources)], refs[len(sources) :]
        grads, outs, left = rest[:2], rest[2 : 2 + size], rest[-1]
        flat = ins[0]
        if turn is not None:
            flat = rest[2 + size]
            turn(*ins, flat)
        chip, core = place()
        plane = lax.axis_index("dp")
        for away in range(size):
            for at in range(other):
                start = (plane ^ away) * chips + at if axis == "dp" else at * chips + (chip ^ away)
                rows = pl.ds(pl.multiple_of((start * 2 + core) * group, group), group)
                target = (away * other + at) * group
                left[target : target + group, :] = flat[rows, :]
        for first in range(columns.start, columns.stop, 512):
            part = slice(first, min(first + 512, columns.stop))
            value = jnp.dot(
                left[:, :row_count], grads[0][:, part], preferred_element_type=jnp.float32
            ) + jnp.dot(left[:, row_count:], grads[1][:, part], preferred_element_type=jnp.float32)
            for away, out in enumerate(outs):
                rows = slice(away * other * group, (away + 1) * other * group)
                out[:, part.start - columns.start : part.stop - columns.start] = value[rows].astype(
                    out.dtype
                )

    width = columns.stop - columns.start
    shapes = [
        jax.ShapeDtypeStruct((other * group, width), jnp.float32 if away == 0 else jnp.bfloat16)
        for away in range(size)
    ]
    if turn is not None:
        shapes.append(target)
    return pl.pallas_call(
        kernel,
        out_shape=shapes,
        in_specs=[VMEM] * (len(sources) + 2),
        out_specs=[VMEM] * len(shapes),
        scratch_shapes=[pltpu.VMEM((size * other * group, 2 * row_count), jnp.bfloat16)],
        compiler_params=params(32),
        cost_estimate=pl.CostEstimate(
            flops=2 * shape[0] * row_count * width,
            bytes_accessed=4 * row_count * width,
            transcendentals=0,
        ),
        name="weight_gradient",
    )(*sources, grad_near, grad_far)


def project(pieces, out_weight, chips, width):
    row_count = pieces[0].shape[0]
    out_width = out_weight.shape[1]

    def kernel(*refs):
        ins, weight, out = refs[:chips], refs[chips], refs[chips + 1]
        chip, _ = place()
        step = min(out_width, 512)
        for column in range(0, out_width, step):
            value = None
            for away in range(chips):
                start = pl.multiple_of((chip ^ away) * width, width)
                part = jnp.dot(
                    ins[away][...],
                    weight[pl.ds(start, width), column : column + step],
                    preferred_element_type=jnp.float32,
                )
                value = part if value is None else value + part
            out[:, column : column + step] = value.astype(out.dtype)

    return pl.pallas_call(
        kernel,
        out_shape=jax.ShapeDtypeStruct((row_count, out_width), jnp.bfloat16),
        in_specs=[VMEM] * (chips + 1),
        out_specs=VMEM,
        compiler_params=params(24),
        cost_estimate=pl.CostEstimate(
            flops=2 * row_count * out_weight.size,
            bytes_accessed=2 * out_weight.size,
            transcendentals=0,
        ),
        name="project",
    )(*pieces, out_weight)


def add_up(own, others, axis, size):
    group = own.shape[0] // size

    def kernel(*refs):
        ins, outs = refs[: 1 + len(others)], refs[1 + len(others) :]
        here = lax.axis_index("dp") if axis == "dp" else place()[0]
        for away in range(size):
            rows = pl.ds(pl.multiple_of((here ^ away) * group, group), group)
            value = ins[0][rows, :]
            for ref in ins[1:]:
                value = value + ref[rows, :].astype(jnp.float32)
            outs[away][...] = value.astype(outs[away].dtype)

    return pl.pallas_call(
        kernel,
        out_shape=[
            jax.ShapeDtypeStruct(
                (group, own.shape[1]), jnp.float32 if away == 0 else jnp.bfloat16
            )
            for away in range(size)
        ],
        in_specs=[VMEM] * (1 + len(others)),
        out_specs=[VMEM] * size,
        compiler_params=params(16),
        name="add_up",
    )(own, *others)


def finish(lefts, rights):
    rows, split = lefts[0].shape
    width = split + rights[0].shape[1]

    def kernel(*refs):
        ins, out = refs[:-1], refs[-1]
        for group, columns in (
            (ins[: len(lefts)], slice(0, split)),
            (ins[len(lefts) :], slice(split, width)),
        ):
            value = group[0][...]
            for ref in group[1:]:
                value = value + ref[...].astype(jnp.float32)
            out[:, columns] = value

    return pl.pallas_call(
        kernel,
        out_shape=jax.ShapeDtypeStruct((rows, width), jnp.float32),
        in_specs=[VMEM] * (len(lefts) + len(rights)),
        out_specs=VMEM,
        compiler_params=params(16),
        name="finish",
    )(*lefts, *rights)


def body(seq, planes, query_rows, key_rows, value_rows, scale_end, out_weight, grad_out):
    chips = seq // 2
    full = query_rows.shape[2]
    width = full // chips

    def over(axis, size, value, mask):
        return lax.ppermute(value, axis, [(i, i ^ mask) for i in range(size)])

    def other_core(value):
        return over("seq", seq, value, 1)

    def spread(pieces):
        return [pieces[0]] + [over("seq", seq, pieces[away], 2 * away) for away in range(1, chips)]

    def meet(pieces):
        return [pieces[0]] + [over("dp", planes, pieces[away], away) for away in range(1, planes)]

    sources = [key_rows[0], value_rows[0]]
    last = cut(sources, [chips - 1], width)
    rest = cut(sources, range(chips - 1), width)
    near = spread([*rest, *last])
    queries = spread(cut([query_rows[0]], range(chips), width))
    ends = spread([scale_end.reshape(-1, HEAD)] * chips)
    far = [other_core(piece) for piece in near]
    grad_near = grad_out[0]
    grad_far = other_core(grad_near)
    both = assemble(near, far, chips)
    mine = [None] * chips
    for aways in ([0], [chips - 1], list(range(1, chips - 1))):
        results = attend(
            [queries[i] for i in aways], [ends[i] for i in aways], both, width
        )
        for away, piece in zip(aways, results):
            mine[away] = over("seq", seq, piece, 2 * away) if away else piece
    others = [other_core(piece) for piece in mine]
    out_width = out_weight.shape[1]
    split = out_width * 11 // 16
    grads = (grad_near, grad_far)
    *by_chip, turned = weight_gradient(
        None, *grads, slice(0, split), "seq", chips, planes, (mine, others, chips, width)
    )
    gathered = spread(by_chip)
    by_plane = weight_gradient(
        turned, *grads, slice(split, out_width), "dp", chips, planes
    )
    met = meet(by_plane)
    mixed_out = project(mine, out_weight, chips, width)[None]
    lefts = meet(add_up(gathered[0], gathered[1:], "dp", planes))
    rights = spread(add_up(met[0], met[1:], "seq", chips))
    return mixed_out, finish(lefts, rights)


def solution(mesh):
    placed = (
        P("dp", "seq", None),
        P("dp", "seq", None),
        P("dp", "seq", None),
        P("seq"),
        P(),
        P("dp", "seq", None),
    )
    seq, planes = mesh.shape["seq"], mesh.shape["dp"]
    return jax.shard_map(
        functools.partial(body, seq, planes),
        mesh=mesh,
        in_specs=placed,
        out_specs=(P("dp", "seq", None), P(("dp", "seq"), None)),
        check_vma=False,
    )
```

```python
import functools

import jax
import jax.numpy as jnp
from jax import lax
from jax.experimental import pallas as pl
from jax.experimental.pallas import tpu as pltpu
from jax.sharding import PartitionSpec as P


HEAD = 128
FLOOR = -1e30
LOG2E = 1.4426950408889634


HBM = pl.BlockSpec(memory_space=pltpu.HBM)
VMEM = pl.BlockSpec(memory_space=pltpu.VMEM)


def place():
    index = lax.axis_index("seq")
    return index // 2, index % 2


def params(mebibytes):
    return pltpu.CompilerParams(vmem_limit_bytes=mebibytes * 1024 * 1024)


def cut(sources, aways, width):
    row_count = sources[0].shape[0]
    count = len(sources)

    def kernel(*refs):
        ins, outs, sems = refs[:count], refs[count:-1], refs[-1]
        chip, _ = place()
        copies = []
        for out, away in zip(outs, aways):
            columns = pl.ds(pl.multiple_of((chip ^ away) * width, width), width)
            for at, source in enumerate(ins):
                copies.append(
                    pltpu.make_async_copy(
                        source.at[:, columns],
                        out.at[:, at * width : (at + 1) * width],
                        sems.at[len(copies)],
                    )
                )
        for copy in copies:
            copy.start()
        for copy in copies:
            copy.wait()

    shape = jax.ShapeDtypeStruct((row_count, count * width), sources[0].dtype)
    return pl.pallas_call(
        kernel,
        out_shape=[shape] * len(aways),
        in_specs=[HBM] * count,
        out_specs=[VMEM] * len(aways),
        scratch_shapes=[pltpu.SemaphoreType.DMA((count * len(aways),))],
        compiler_params=params(16),
        name="cut",
    )(*(pltpu.with_memory_space_constraint(source, pltpu.HBM) for source in sources))


def assemble(near, far, chips):
    row_count, wide = near[0].shape

    def kernel(*refs):
        pieces, out = (refs[:chips], refs[chips : 2 * chips]), refs[2 * chips]
        chip, core = place()
        for away in range(chips):
            for side in range(2):
                at = (chip ^ away) * 2 + (core ^ side)
                rows = pl.ds(pl.multiple_of(at * row_count, row_count), row_count)
                out[rows, :] = pieces[side][away][...]

    return pl.pallas_call(
        kernel,
        out_shape=jax.ShapeDtypeStruct((2 * chips * row_count, wide), near[0].dtype),
        in_specs=[VMEM] * (2 * chips),
        out_specs=VMEM,
        compiler_params=params(16),
        name="assemble",
    )(*near, *far)


def attend(queries, ends, both, width):
    row_count = queries[0].shape[0]
    total = both.shape[0]
    heads = width // HEAD
    count = len(queries)
    step_k = total // 4
    scale = float(HEAD) ** -0.5 * LOG2E

    def kernel(*refs):
        ends_in = refs[:count]
        q_in = refs[count : 2 * count]
        both_ref = refs[2 * count]
        outs = refs[2 * count + 1 : 3 * count + 1]
        qbuf, obuf, sbuf, sums, tallies, tops = refs[3 * count + 1 :]

        def part(index, room, base, steps):
            shifts, factors = [], []
            for head in range(heads):
                columns = slice(head * HEAD, (head + 1) * HEAD)
                query = q_in[0][:, columns] if count == 1 else qbuf[index, :, columns]
                top = None
                for at in range(base, base + steps * step_k, step_k):
                    score = lax.dot_general(
                        query,
                        both_ref[at : at + step_k, columns],
                        (((1,), (1,)), ((), ())),
                        preferred_element_type=jnp.float32,
                    )
                    for key in range(0, step_k, HEAD):
                        piece = jnp.where(room > at + key, score[:, key : key + HEAD], FLOOR)
                        sbuf[head, :, at - base + key : at - base + key + HEAD] = piece
                        top = piece if top is None else jnp.maximum(top, piece)
                shift = jnp.broadcast_to(jnp.max(top, axis=1, keepdims=True), top.shape) * scale
                if base:
                    before = tops[head]
                    shift = jnp.maximum(before, shift)
                    factors.append(jnp.exp2(before - shift))
                shifts.append(shift)
            for head in range(heads):
                tally = acc = None
                for at in range(base, base + steps * step_k, step_k):
                    weights = []
                    for key in range(0, step_k, HEAD):
                        piece = sbuf[head, :, at - base + key : at - base + key + HEAD]
                        piece = jnp.exp2(piece * scale - shifts[head])
                        tally = piece if tally is None else tally + piece
                        weights.append(piece.astype(jnp.bfloat16))
                    product = jnp.dot(
                        jnp.concatenate(weights, axis=1),
                        both_ref[at : at + step_k, width + head * HEAD : width + (head + 1) * HEAD],
                        preferred_element_type=jnp.float32,
                    )
                    acc = product if acc is None else acc + product
                if base:
                    acc = acc + sums[head] * factors[head]
                    tally = tally + tallies[head] * factors[head]
                sums[head], tallies[head], tops[head] = acc, tally, shifts[head]

        for index in range(count):
            if count > 1:
                qbuf[index] = q_in[index][...]

        def turn(index, carry):
            end = ends_in[0][...]
            for at in range(1, count):
                end = jnp.where(index == at, ends_in[at][...], end)
            end = end.astype(jnp.float32)
            reach = jnp.max(end)
            bound = jnp.concatenate(
                [
                    jnp.broadcast_to(end[at : at + 1], (HEAD, HEAD)).T
                    for at in range(row_count // HEAD)
                ],
                axis=0,
            )
            lane = lax.broadcasted_iota(jnp.int32, (row_count, HEAD), 1)
            room = bound - lane.astype(jnp.float32)
            for test, base, steps in (
                (reach <= step_k, 0, 1),
                (reach > step_k, 0, 2),
                ((reach > 2 * step_k) & (reach <= 3 * step_k), 2 * step_k, 1),
                (reach > 3 * step_k, 2 * step_k, 2),
            ):

                @pl.when(test)
                def _(base=base, steps=steps):
                    part(index, room, base, steps)

            for head in range(heads):
                value = sums[head] / jnp.sum(tallies[head], axis=1, keepdims=True)
                columns = slice(head * HEAD, (head + 1) * HEAD)
                if count == 1:
                    outs[0][:, columns] = value.astype(obuf.dtype)
                else:
                    obuf[index, :, columns] = value.astype(obuf.dtype)
            return carry

        if count == 1:
            turn(0, 0)
            return
        lax.fori_loop(0, count, turn, 0)
        for index in range(count):
            outs[index][...] = obuf[index]

    state = pltpu.VMEM((heads, row_count, HEAD), jnp.float32)
    return pl.pallas_call(
        kernel,
        out_shape=[jax.ShapeDtypeStruct((row_count, width), jnp.bfloat16)] * count,
        in_specs=[VMEM] * (2 * count + 1),
        out_specs=[VMEM] * count,
        scratch_shapes=[
            pltpu.VMEM((count, row_count, width), jnp.bfloat16),
            pltpu.VMEM((count, row_count, width), jnp.bfloat16),
            pltpu.VMEM((heads, row_count, total // 2), jnp.float32),
            state,
            state,
            state,
        ],
        compiler_params=params(30),
        cost_estimate=pl.CostEstimate(
            flops=4 * count * row_count * total * width,
            bytes_accessed=4 * total * width,
            transcendentals=count * row_count * total * heads,
        ),
        name="attend",
    )(*ends, *queries, both)


def turning(pieces, chips, width):
    row_count = pieces[0].shape[0]

    def kernel(*refs):
        ins, out = refs[:chips], refs[chips]
        chip, _ = place()
        for away in range(chips):
            start = pl.multiple_of((chip ^ away) * width, width)
            out[pl.ds(start, width), :] = ins[away][...].T

    return kernel, jax.ShapeDtypeStruct((chips * width, row_count), pieces[0].dtype)


def turn_over(pieces, chips, width):
    kernel, shape = turning(pieces, chips, width)
    return pl.pallas_call(
        kernel,
        out_shape=shape,
        in_specs=[VMEM] * chips,
        out_specs=VMEM,
        compiler_params=params(16),
        name="turn_over",
    )(*pieces)


def weight_gradient(near, far, grad_near, grad_far, columns, axis, chips, planes, pieces=None):
    row_count = grad_near.shape[0]
    if pieces is None:
        turn, sources = None, [near, far]
    else:
        turn, target = turning(*pieces)
        sources = [near, *pieces[0]]
    group = near.shape[0] // (planes * chips * 2)
    size = planes if axis == "dp" else chips
    other = chips if axis == "dp" else planes

    def kernel(*refs):
        ins, rest = refs[: len(sources)], refs[len(sources) :]
        grads, outs, left = rest[:2], rest[2 : 2 + size], rest[-1]
        flat = ins[:2]
        if turn is not None:
            flat = (ins[0], rest[2 + size])
            turn(*ins[1:], flat[1])
        chip, core = place()
        plane = lax.axis_index("dp")
        for away in range(size):
            for at in range(other):
                start = (plane ^ away) * chips + at if axis == "dp" else at * chips + (chip ^ away)
                rows = pl.ds(pl.multiple_of((start * 2 + core) * group, group), group)
                target = (away * other + at) * group
                for side in range(2):
                    left[
                        target : target + group, side * row_count : (side + 1) * row_count
                    ] = flat[side][rows, :]
        for first in range(columns.start, columns.stop, 512):
            part = slice(first, min(first + 512, columns.stop))
            value = jnp.dot(
                left[:, :row_count], grads[0][:, part], preferred_element_type=jnp.float32
            ) + jnp.dot(left[:, row_count:], grads[1][:, part], preferred_element_type=jnp.float32)
            for away, out in enumerate(outs):
                rows = slice(away * other * group, (away + 1) * other * group)
                out[:, part.start - columns.start : part.stop - columns.start] = value[rows].astype(
                    out.dtype
                )

    width = columns.stop - columns.start
    shapes = [
        jax.ShapeDtypeStruct((other * group, width), jnp.float32 if away == 0 else jnp.bfloat16)
        for away in range(size)
    ]
    if turn is not None:
        shapes.append(target)
    return pl.pallas_call(
        kernel,
        out_shape=shapes,
        in_specs=[VMEM] * (len(sources) + 2),
        out_specs=[VMEM] * len(shapes),
        scratch_shapes=[pltpu.VMEM((size * other * group, 2 * row_count), jnp.bfloat16)],
        compiler_params=params(32),
        cost_estimate=pl.CostEstimate(
            flops=2 * near.shape[0] * row_count * width,
            bytes_accessed=4 * row_count * width,
            transcendentals=0,
        ),
        name="weight_gradient",
    )(*sources, grad_near, grad_far)


def project(pieces, out_weight, chips, width):
    row_count = pieces[0].shape[0]
    out_width = out_weight.shape[1]

    def kernel(*refs):
        ins, weight, out = refs[:chips], refs[chips], refs[chips + 1]
        chip, _ = place()
        step = min(out_width, 512)
        for column in range(0, out_width, step):
            value = None
            for away in range(chips):
                start = pl.multiple_of((chip ^ away) * width, width)
                part = jnp.dot(
                    ins[away][...],
                    weight[pl.ds(start, width), column : column + step],
                    preferred_element_type=jnp.float32,
                )
                value = part if value is None else value + part
            out[:, column : column + step] = value.astype(out.dtype)

    return pl.pallas_call(
        kernel,
        out_shape=jax.ShapeDtypeStruct((row_count, out_width), jnp.bfloat16),
        in_specs=[VMEM] * (chips + 1),
        out_specs=VMEM,
        compiler_params=params(24),
        cost_estimate=pl.CostEstimate(
            flops=2 * row_count * out_weight.size,
            bytes_accessed=2 * out_weight.size,
            transcendentals=0,
        ),
        name="project",
    )(*pieces, out_weight)


def add_up(own, others, axis, size):
    group = own.shape[0] // size

    def kernel(*refs):
        ins, outs = refs[: 1 + len(others)], refs[1 + len(others) :]
        here = lax.axis_index("dp") if axis == "dp" else place()[0]
        for away in range(size):
            rows = pl.ds(pl.multiple_of((here ^ away) * group, group), group)
            value = ins[0][rows, :]
            for ref in ins[1:]:
                value = value + ref[rows, :].astype(jnp.float32)
            outs[away][...] = value.astype(outs[away].dtype)

    return pl.pallas_call(
        kernel,
        out_shape=[
            jax.ShapeDtypeStruct(
                (group, own.shape[1]), jnp.float32 if away == 0 else jnp.bfloat16
            )
            for away in range(size)
        ],
        in_specs=[VMEM] * (1 + len(others)),
        out_specs=[VMEM] * size,
        compiler_params=params(16),
        name="add_up",
    )(own, *others)


def finish(lefts, rights):
    rows, split = lefts[0].shape
    width = split + rights[0].shape[1]

    def kernel(*refs):
        ins, out = refs[:-1], refs[-1]
        for group, columns in (
            (ins[: len(lefts)], slice(0, split)),
            (ins[len(lefts) :], slice(split, width)),
        ):
            value = group[0][...]
            for ref in group[1:]:
                value = value + ref[...].astype(jnp.float32)
            out[:, columns] = value

    return pl.pallas_call(
        kernel,
        out_shape=jax.ShapeDtypeStruct((rows, width), jnp.float32),
        in_specs=[VMEM] * (len(lefts) + len(rights)),
        out_specs=VMEM,
        compiler_params=params(16),
        name="finish",
    )(*lefts, *rights)


def body(seq, planes, query_rows, key_rows, value_rows, scale_end, out_weight, grad_out):
    chips = seq // 2
    full = query_rows.shape[2]
    width = full // chips

    def over(axis, size, value, mask):
        return lax.ppermute(value, axis, [(i, i ^ mask) for i in range(size)])

    def other_core(value):
        return over("seq", seq, value, 1)

    def spread(pieces):
        return [pieces[0]] + [over("seq", seq, pieces[away], 2 * away) for away in range(1, chips)]

    def meet(pieces):
        return [pieces[0]] + [over("dp", planes, pieces[away], away) for away in range(1, planes)]

    sources = [key_rows[0], value_rows[0]]
    last = cut(sources, [chips - 1], width)
    rest = cut(sources, range(chips - 1), width)
    near = spread([*rest, *last])
    queries = spread(cut([query_rows[0]], range(chips), width))
    ends = spread([scale_end.reshape(-1, HEAD)] * chips)
    far = [other_core(piece) for piece in near]
    grad_near = grad_out[0]
    grad_far = other_core(grad_near)
    both = assemble(near, far, chips)
    mine = [None] * chips
    for aways in ([chips - 1], list(range(1, chips - 1)), [0]):
        results = attend(
            [queries[i] for i in aways], [ends[i] for i in aways], both, width
        )
        for away, piece in zip(aways, results):
            mine[away] = over("seq", seq, piece, 2 * away) if away else piece
    others = [other_core(piece) for piece in mine]
    out_width = out_weight.shape[1]
    split = out_width * 11 // 16
    grads = (grad_near, grad_far)
    turned = turn_over(mine, chips, width)
    *by_chip, far_turned = weight_gradient(
        turned, None, *grads, slice(0, split), "seq", chips, planes, (others, chips, width)
    )
    gathered = spread(by_chip)
    by_plane = weight_gradient(
        turned, far_turned, *grads, slice(split, out_width), "dp", chips, planes
    )
    met = meet(by_plane)
    mixed_out = project(mine, out_weight, chips, width)[None]
    lefts = meet(add_up(gathered[0], gathered[1:], "dp", planes))
    rights = spread(add_up(met[0], met[1:], "seq", chips))
    return mixed_out, finish(lefts, rights)


def solution(mesh):
    placed = (
        P("dp", "seq", None),
        P("dp", "seq", None),
        P("dp", "seq", None),
        P("seq"),
        P(),
        P("dp", "seq", None),
    )
    seq, planes = mesh.shape["seq"], mesh.shape["dp"]
    return jax.shard_map(
        functools.partial(body, seq, planes),
        mesh=mesh,
        in_specs=placed,
        out_specs=(P("dp", "seq", None), P(("dp", "seq"), None)),
        check_vma=False,
    )
```
